32 devices in a mesh: grp: 2 (over y), req: 8 (over z, x), head: 2 (over core).
Axes of the slice: x: 2, y: 2, z: 4, core: 2. Of those that a mesh axis runs over, the one named last changes fastest.
Arguments:
- draft_input: bfloat16 [1024, 8192], P(('grp', 'req'), 'head'), parts along dimension 0, may hold values from -4.5 to 4.5
- draft_proj: bfloat16 [1024, 2048], P(('grp', 'req'), 'head'), parts along dimension 0, may hold values from -4.5 to 4.5
- draft_step: bfloat16 [1024, 128], P(('grp', 'req'), 'head'), parts along dimension 0, may hold values from -4 to 4
- draft_query: bfloat16 [1024, 4096], P(('grp', 'req'), 'head'), parts along dimension 0, may hold values from -120 to 120
- draft_keyval: bfloat16 [1024, 1024], P(('grp', 'req'), 'head'), parts along dimension 0, may hold values from -4.5 to 4.5
- row_target: int32 [1024], P(('grp', 'req')), parts along dimension 0, may hold values from 0 to 511, as said below
- tree_mask: int32 [16, 64, 64], P(('grp', 'req')), parts along dimension 0, may hold values from 0 to 1, as said below
- accepted: int32 [16], P(('grp', 'req')), parts along dimension 0, may hold values from 0 to 63
- cache_length: int32 [16], P(('grp', 'req')), parts along dimension 0, may hold values from 1 to 1024, as said below
- scan_state: bfloat16 [16, 128, 64, 128], P(('grp', 'req'), 'head'), parts along dimension 0, may hold values from -10.5 to 10.5
- cache_keyval: bfloat16 [16, 1024, 1024], P(('grp', 'req'), None, 'head'), parts along dimension 0, may hold values from -4.5 to 4.5
- decay_rate: float32 [128], P('head'), may hold values from 0.02 to 1.5
- step_bias: float32 [128], P('head'), may hold values from -3.5 to -1.5
- skip_gain: float32 [128], P('head'), may hold values from 0.5 to 1.5
- norm_gain: float32 [8192], P('head'), may hold values from 0.5 to 1.5
Outputs:
- mixer_out: bfloat16 [1024, 8192], P(('grp', 'req'), 'head'), parts along dimension 0
- attend_out: bfloat16 [1024, 4096], P(('grp', 'req'), 'head'), parts along dimension 0
- accepted_state: bfloat16 [16, 128, 64, 128], P(('grp', 'req'), 'head'), parts along dimension 0
The draws below stay inside these ranges and needn't reach their ends.
There are 2 independent parts, one for each index of `grp`. The reference program is written for one: setup_inputs(seed, part) draws one part's arguments, and reference() takes and returns one part's arrays. A program takes and returns all parts, laid end to end along the dimension named above; an argument that names none is the same for every part. Nothing has to cross between parts.
Inputs may be any that keep to these rules, and one draw needn't show every extreme that they name: `row_target`: A permutation of all rows. The owner of row g is g // 64. Of the 64 rows of one drafter device at most 8 go to any one owner, and some drafter sends exactly 8 to some owner. tree_mask[r,i,j] is 1 exactly when node j is node i or an ancestor of node i; node 0 is the root and every parent has a smaller index than its child. `cache_length`: some request uses all 1024 positions.
All inputs are finite; a program needn't handle non-finite values.
Results may differ from the reference program's by a relative error of at most 0.0049.
Values may be sent and summed in bfloat16 or wider, within the bound.
No kernel may reach another device: no remote copies, remote signals or barrier semaphores. Data moves between devices by JAX's collectives and lax.ppermute only.
A program may use at most 128 MiB of HBM per device.

```python
import math
import jax
import jax.numpy as jnp
from jax import lax

HEADS = 128
HEAD_DIM = 64
STATE = 128
GROUPS = 8
QHEADS = 32
KVHEADS = 4
QDIM = 128
NODES = 64
KV_MAX = 1024
ROWS_DEV = 64
REQS = 8
ROWS = 512
MOST = 8
N_REQ = 8


def draw_row_target(key, part):
    owners = N_REQ
    group_count = ROWS_DEV // MOST
    key_shift, key_owner, key_drafter = jax.random.split(key, 3)
    shift_of = jax.random.permutation(key_shift, owners)[:group_count]

    def shuffle(one_key):
        return jax.random.permutation(one_key, ROWS_DEV)
    owner_perm = jax.vmap(shuffle)(jax.random.split(key_owner, owners))
    drafter_perm = jax.vmap(shuffle)(jax.random.split(key_drafter, owners))
    drafter_ids = jnp.arange(owners)[:, None, None]
    group_ids = jnp.arange(group_count)[None, :, None]
    within = jnp.arange(MOST)[None, None, :]
    source_owner = (drafter_ids - shift_of[group_ids]) % owners
    owner_slot = owner_perm[source_owner, group_ids * MOST + within]
    drafter_slot = drafter_perm[drafter_ids, group_ids * MOST + within]
    position = (drafter_ids * ROWS_DEV + drafter_slot).reshape(-1)
    target = (source_owner * ROWS_DEV + owner_slot).reshape(-1)
    return jnp.zeros((ROWS,), jnp.int32).at[position].set(target.astype(jnp.int32))


def draw_tree_mask(key, part):
    offsets = jax.random.randint(key, (REQS, NODES), 1, 5)
    node_ids = jnp.arange(NODES)
    parents = jnp.maximum(node_ids[None, :] - offsets, 0).astype(jnp.int32)
    identity = jnp.eye(NODES, dtype=jnp.int32)

    def one_tree(parent_row):

        def add_node(node_index, ancestry):
            return ancestry.at[node_index].set(ancestry[parent_row[node_index]] + identity[node_index])
        return lax.fori_loop(1, NODES, add_node, identity)
    return jax.vmap(one_tree)(parents)


def draw_accepted(key, part):
    key_value, key_spot = jax.random.split(key)
    values = jax.random.randint(key_value, (REQS,), 0, NODES)
    special = jax.random.permutation(key_spot, REQS)
    return values.at[special[0]].set(NODES - 1).at[special[1]].set(0).astype(jnp.int32)


def draw_cache_length(key, part):
    key_first, key_second, key_spot = jax.random.split(key, 3)
    first_draw = jax.random.randint(key_first, (REQS,), 1, KV_MAX + 1)
    second_draw = jax.random.randint(key_second, (REQS,), 1, KV_MAX + 1)
    lengths = jnp.maximum(first_draw * second_draw // KV_MAX, 1)
    special = jax.random.randint(key_spot, (), 0, REQS)
    return lengths.at[special].set(KV_MAX).astype(jnp.int32)


def draw_scan_state(key, part):
    shape_all = (REQS, HEADS, HEAD_DIM, STATE)
    head_ramp = jnp.arange(HEADS, dtype=jnp.float32) / max(HEADS - 1, 1)
    head_scale = 0.5 * 4.0 ** head_ramp
    base_draw = jnp.clip(jax.random.normal(key, shape_all, jnp.float32), -4.0, 4.0)
    return (base_draw * head_scale[None, :, None, None]).astype(jnp.bfloat16)


def keyval_base(key):
    return jnp.clip(jax.random.normal(jax.random.fold_in(key, 17), (ROWS, KVHEADS, 2, QDIM), jnp.float32), -4.5, 4.5)


def draw_draft_keyval(key, part):
    return keyval_base(key).reshape(ROWS, KVHEADS * 2 * QDIM).astype(jnp.bfloat16)


def draw_draft_query(key, part):
    group_size = QHEADS // KVHEADS
    base_draw = jnp.clip(jax.random.normal(jax.random.fold_in(key, 29), (ROWS, KVHEADS, group_size, QDIM), jnp.float32), -4.5, 4.5)
    return base_draw.reshape(ROWS, QHEADS * QDIM).astype(jnp.bfloat16)


def shard_levels(own_key, shape, cuts, smallest, top_value):
    def one(dim, shards_of):
        steps = jax.random.uniform(jax.random.fold_in(jax.random.fold_in(own_key, 6), dim), (shards_of,), jnp.float32, smallest / len(cuts), top_value / len(cuts))
        return jnp.repeat(jnp.exp(steps), shape[dim] // shards_of).reshape((-1,) + (1,) * (len(shape) - dim - 1))

    factor_of = one(*cuts[0])
    for cut in cuts[1:]:
        factor_of = factor_of * one(*cut)
    return factor_of


def centred(own_key, dims, width, most, shards=(), held_as=jnp.bfloat16):
    entries = width * jax.random.normal(own_key, dims, jnp.float32)
    if shards:
        entries = entries * shard_levels(own_key, dims, shards, -0.22, 0.18)
    return jnp.clip(entries, -most, most).astype(held_as)


def setup_inputs(seed: int = 0, part: int = 0) -> dict:
    seeds = jax.random.split(jax.random.key(seed), 16)
    part_splits = jax.random.split(jax.random.fold_in(seeds[15], part), 16)
    draft_input = centred(part_splits[0], (ROWS, HEADS * HEAD_DIM), 1.0, 4.5, ((0, 8), (1, 2)))
    draft_proj = centred(part_splits[1], (ROWS, GROUPS * 2 * STATE), 1.0, 4.5, ((0, 8), (1, 2)))
    draft_step = centred(part_splits[2], (ROWS, HEADS), 1.0, 4.0, ((0, 8), (1, 2)))
    draft_query = draw_draft_query(jax.random.fold_in(jax.random.fold_in(seeds[15], part), 71), part)
    draft_keyval = draw_draft_keyval(jax.random.fold_in(jax.random.fold_in(seeds[15], part), 71), part)
    row_target = draw_row_target(jax.random.fold_in(jax.random.fold_in(seeds[15], part), 71), part)
    tree_mask = draw_tree_mask(jax.random.fold_in(jax.random.fold_in(seeds[15], part), 71), part)
    accepted = draw_accepted(jax.random.fold_in(jax.random.fold_in(seeds[15], part), 71), part)
    cache_length = draw_cache_length(jax.random.fold_in(jax.random.fold_in(seeds[15], part), 71), part)
    scan_state = draw_scan_state(jax.random.fold_in(jax.random.fold_in(seeds[15], part), 71), part)
    cache_keyval = centred(part_splits[10], (REQS, KV_MAX, KVHEADS * 2 * QDIM), 1.0, 4.5, ((0, 8), (2, 2)))
    decay_rate = jnp.clip(jnp.exp(math.log(1.5) - 4.317488 * jax.random.uniform(seeds[11], (HEADS,), jnp.float32) ** shard_levels(seeds[11], (HEADS,), ((0, 2),), -0.2, 0.2)), 0.02, 1.5)
    step_bias = jnp.clip(-3.5 + 2.0 * jax.random.uniform(seeds[12], (HEADS,), jnp.float32) ** shard_levels(seeds[12], (HEADS,), ((0, 2),), -0.2, 0.2), -3.5, -1.5)
    skip_gain = jnp.clip(0.5 + 1.0 * jax.random.uniform(seeds[13], (HEADS,), jnp.float32) ** shard_levels(seeds[13], (HEADS,), ((0, 2),), -0.2, 0.2), 0.5, 1.5)
    norm_gain = jnp.clip(1.0 + 0.1 * jax.random.normal(seeds[14], (HEADS * HEAD_DIM,), jnp.float32), 0.5, 1.5)
    return {"draft_input": draft_input, "draft_proj": draft_proj, "draft_step": draft_step, "draft_query": draft_query, "draft_keyval": draft_keyval, "row_target": row_target, "tree_mask": tree_mask, "accepted": accepted, "cache_length": cache_length, "scan_state": scan_state, "cache_keyval": cache_keyval, "decay_rate": decay_rate, "step_bias": step_bias, "skip_gain": skip_gain, "norm_gain": norm_gain}


def tree_scan(features, proj_pairs, raw_step, mask_rows, accepted_node, state_one, decay_rate, step_bias, skip_gain):
    node_count, head_count, head_width = features.shape
    group_count = proj_pairs.shape[1]
    per_group = head_count // group_count
    mask_float = mask_rows.astype(jnp.float32)
    step_size = jax.nn.softplus(raw_step.astype(jnp.float32) + step_bias[None, :])
    cumulative = jnp.dot(mask_float, -decay_rate[None, :] * step_size, precision=lax.Precision.HIGHEST)
    write_rows = proj_pairs[:, :, 0, :].astype(jnp.float32)
    read_rows = proj_pairs[:, :, 1, :].astype(jnp.float32)
    inner_prod = jnp.einsum('ign,jgn->gij', read_rows, write_rows)
    inner_prod = jnp.repeat(inner_prod, per_group, axis=0)
    cumulative_heads = cumulative.T
    weight = mask_float[None] * jnp.exp(jnp.minimum(cumulative_heads[:, :, None] - cumulative_heads[:, None, :], 0.0))
    weight = (weight * inner_prod * step_size.T[:, None, :]).astype(jnp.bfloat16)
    features_wide = features.astype(jnp.float32)
    intra_part = jnp.einsum('hij,jhp->ihp', weight.astype(jnp.float32), features_wide)
    state_groups = state_one.astype(jnp.float32).reshape(group_count, per_group, head_width, -1)
    carried = jnp.einsum('ign,gqpn->igqp', read_rows, state_groups).reshape(node_count, head_count, head_width)
    mixed_rows = intra_part + jnp.exp(cumulative)[:, :, None] * carried + skip_gain[None, :, None] * features_wide
    chosen = (lax.iota(jnp.int32, node_count) == accepted_node).astype(jnp.float32)
    cumulative_pick = jnp.dot(chosen, cumulative, precision=lax.Precision.HIGHEST)
    mask_pick = jnp.dot(chosen, mask_float, precision=lax.Precision.HIGHEST)
    path_weight = mask_pick[:, None] * jnp.exp(jnp.minimum(cumulative_pick[None, :] - cumulative, 0.0)) * step_size
    weighted = (path_weight[:, :, None] * features_wide).astype(jnp.bfloat16)
    weighted = weighted.reshape(node_count, group_count, per_group, head_width).astype(jnp.float32)
    update = jnp.einsum('jgqp,jgn->gqpn', weighted, write_rows).reshape(head_count, head_width, -1)
    new_state = (jnp.exp(cumulative_pick)[:, None, None] * state_one.astype(jnp.float32) + update).astype(jnp.bfloat16)
    return (mixed_rows, new_state)

def attend(queries, tree_pairs, cache_pairs, length, mask_rows):
    node_count = queries.shape[0]
    cache_count = cache_pairs.shape[0]
    query_scale = queries.shape[-1] ** (-0.5)
    query_wide = queries.astype(jnp.float32)
    cache_scores = jnp.einsum('ikgd,pkd->kgip', query_wide, cache_pairs[:, :, 0, :].astype(jnp.float32)) * query_scale
    tree_scores = jnp.einsum('ikgd,jkd->kgij', query_wide, tree_pairs[:, :, 0, :].astype(jnp.float32)) * query_scale
    valid_cache = lax.iota(jnp.int32, cache_count) < length
    cache_scores = jnp.where(valid_cache[None, None, None, :], cache_scores, -1e+30)
    tree_scores = jnp.where(mask_rows[None, None] > 0, tree_scores, -1e+30)
    row_peak = jnp.maximum(lax.optimization_barrier(jnp.max(cache_scores, axis=-1)), lax.optimization_barrier(jnp.max(tree_scores, axis=-1)))[..., None]
    cache_exp = jnp.exp(cache_scores - row_peak)
    tree_exp = jnp.exp(tree_scores - row_peak)
    denominator = (lax.optimization_barrier(jnp.sum(cache_exp, axis=-1)) + lax.optimization_barrier(jnp.sum(tree_exp, axis=-1)))[..., None]
    cache_prob = (cache_exp / denominator).astype(jnp.bfloat16).astype(jnp.float32)
    tree_prob = (tree_exp / denominator).astype(jnp.bfloat16).astype(jnp.float32)
    result = jnp.einsum('kgip,pkd->ikgd', cache_prob, cache_pairs[:, :, 1, :].astype(jnp.float32))
    result = result + jnp.einsum('kgij,jkd->ikgd', tree_prob, tree_pairs[:, :, 1, :].astype(jnp.float32))
    return result.reshape(node_count, -1).astype(jnp.bfloat16)

def reference(draft_input, draft_proj, draft_step, draft_query, draft_keyval, row_target, tree_mask, accepted, cache_length, scan_state, cache_keyval, decay_rate, step_bias, skip_gain, norm_gain):

    def to_owner(draft_rows):
        return jnp.zeros_like(draft_rows).at[row_target].set(draft_rows)
    features = to_owner(draft_input).reshape(REQS, NODES, HEADS, HEAD_DIM)
    proj_pairs = to_owner(draft_proj).reshape(REQS, NODES, GROUPS, 2, STATE)
    raw_step = to_owner(draft_step).reshape(REQS, NODES, HEADS)
    queries = to_owner(draft_query).reshape(REQS, NODES, KVHEADS, QHEADS // KVHEADS, QDIM)
    tree_pairs = to_owner(draft_keyval).reshape(REQS, NODES, KVHEADS, 2, QDIM)
    cached = cache_keyval.reshape(REQS, KV_MAX, KVHEADS, 2, QDIM)
    gain_heads = norm_gain.reshape(HEADS, HEAD_DIM)

    def per_request(request_items):
        one_features, one_pairs, one_step, one_query, one_tree, one_mask, one_pick, one_length, one_state, one_cache = request_items
        mixed_rows, new_state = tree_scan(one_features, one_pairs, one_step, one_mask, one_pick, one_state, decay_rate, step_bias, skip_gain)
        square_sum = lax.optimization_barrier(jnp.sum(mixed_rows * mixed_rows, axis=(1, 2)))
        scale_row = 1.0 / jnp.sqrt(square_sum / (HEADS * HEAD_DIM) + 1e-05)
        normed = (mixed_rows * scale_row[:, None, None] * gain_heads[None]).astype(jnp.bfloat16)
        attended = attend(one_query, one_tree, one_cache, one_length, one_mask)
        return (normed.reshape(NODES, HEADS * HEAD_DIM), attended, new_state)
    mixer_out, attend_out, accepted_state = lax.map(per_request, (features, proj_pairs, raw_step, queries, tree_pairs, tree_mask, accepted, cache_length, scan_state, cached))
    return (mixer_out.reshape(ROWS, HEADS * HEAD_DIM), attend_out.reshape(ROWS, QHEADS * QDIM), accepted_state)
```

```python
import functools

import jax
import jax.numpy as jnp
from jax import lax
from jax.experimental import pallas as pl
from jax.experimental.pallas import tpu as pltpu
from jax.sharding import PartitionSpec as P

HEAD_DIM = 64
STATE = 128
QDIM = 128
NODES = 64
LANES = 128
PAIR = LANES // HEAD_DIM
F32 = jnp.float32
BF16 = jnp.bfloat16


def last_dot(left, right):
    return lax.dot_general(left, right, (((1,), (1,)), ((), ())), preferred_element_type=F32)


def row_to_column(row):
    size = row.shape[1]
    sub = lax.broadcasted_iota(jnp.int32, (size, size), 0)
    lane = lax.broadcasted_iota(jnp.int32, (size, size), 1)
    spread = jnp.broadcast_to(row, (size, size))
    return jnp.sum(jnp.where(sub == lane, spread, jnp.zeros_like(spread)), axis=1, keepdims=True)


def slot_one_hot(target, row_count, cap_rows, slot_total, me):
    shift = row_count.bit_length() - 1
    peer = lax.shift_right_logical(target, jnp.full_like(target, shift))
    local = target - peer * row_count
    peer_f = peer.astype(F32)
    peer_col = row_to_column(peer_f)
    size = row_count
    sub = lax.broadcasted_iota(jnp.int32, (size, size), 0)
    lane = lax.broadcasted_iota(jnp.int32, (size, size), 1)
    same = jnp.logical_and(peer_col == peer_f, sub < lane)
    rank = jnp.sum(jnp.where(same, 1.0, 0.0), axis=0, keepdims=True).astype(jnp.int32)
    block = peer if me is None else jnp.bitwise_xor(peer, jnp.full_like(peer, me))
    slot = block * cap_rows + rank
    slots = lax.broadcasted_iota(jnp.int32, (slot_total, size), 0)
    return jnp.where(slots == slot, 1.0, 0.0).astype(BF16), local


def pack_first(row_count, cap_rows, block_count, xor_blocks, *refs):
    (target_ref, query_ref, keyval_ref, proj_ref, step_ref), outs = refs[:5], refs[5:]
    me = lax.axis_index("req") if xor_blocks else None
    slot_total = block_count * cap_rows
    chosen, local = slot_one_hot(target_ref[...], row_count, cap_rows, slot_total, me)
    local_col = row_to_column((local + 1).astype(F32))
    labels = jnp.broadcast_to(local_col, (row_count, LANES - step_ref.shape[1])).astype(BF16)
    last = jnp.concatenate([step_ref[...], labels], axis=1)
    column = 0
    for part in (query_ref[...], keyval_ref[...], proj_ref[...], last):
        width = part.shape[1]
        moved = jnp.dot(chosen, part, preferred_element_type=F32).astype(BF16)
        put_blocks(outs, moved, slot_total, column, width)
        column += width


def put_blocks(outs, moved, slot_total, column, width):
    rows = slot_total // len(outs)
    for index, out_ref in enumerate(outs):
        out_ref[:, column : column + width] = moved[index * rows : (index + 1) * rows]


def pack_second(row_count, cap_rows, block_count, xor_blocks, *refs):
    (target_ref, input_ref), outs = refs[:2], refs[2:]
    me = lax.axis_index("req") if xor_blocks else None
    slot_total = block_count * cap_rows
    chosen, _ = slot_one_hot(target_ref[...], row_count, cap_rows, slot_total, me)
    moved = jnp.dot(chosen, input_ref[...], preferred_element_type=F32).astype(BF16)
    put_blocks(outs, moved, slot_total, 0, moved.shape[1])


def joined(refs, start, width):
    parts = [ref[:, start : start + width] for ref in refs]
    return parts[0] if len(parts) == 1 else jnp.concatenate(parts, axis=0)


def middle(block_refs, reorder, cap_rows, sizes, *refs):
    query_width, keyval_width, proj_width, head_local = sizes
    blocks, refs = refs[:block_refs], refs[block_refs:]
    (
        accepted_ref,
        length_ref,
        mask_ref,
        state_ref,
        cache_ref,
        decay_ref,
        bias_ref,
        skip_ref,
        attend_ref,
        weight_ref,
        base_ref,
        path_ref,
        keep_ref,
        write_ref,
        order_ref,
        skip_out_ref,
        score_ref,
        prob_ref,
    ) = refs
    nodes = mask_ref.shape[1]
    kv_start = query_width
    proj_start = kv_start + keyval_width
    step_start = proj_start + proj_width
    mask_float = mask_ref[0].astype(F32)
    tail = joined(blocks, step_start, LANES)
    label_lane = tail[:, LANES - nodes :].astype(F32)
    slot_total = tail.shape[0]
    node_lane = lax.broadcasted_iota(jnp.int32, (slot_total, nodes), 1).astype(F32) + 1.0
    order = jnp.where(label_lane == node_lane, 1.0, 0.0).T.astype(BF16)
    order_ref[...] = order

    def ordered(start, width):
        return jnp.dot(order, joined(blocks, start, width), preferred_element_type=F32)

    pair_heads = keyval_width // (2 * QDIM)
    group_size = query_width // QDIM // pair_heads
    cache_count = cache_ref.shape[1]
    query_scale = QDIM ** (-0.5)
    length = length_ref[0]
    valid = lax.broadcasted_iota(jnp.int32, (1, cache_count), 1) < length
    tree_valid = mask_float > 0.0
    tree_pairs = ordered(kv_start, keyval_width).astype(BF16)
    for pair in range(pair_heads):
        first = pair * group_size * QDIM
        query = ordered(first, group_size * QDIM).astype(BF16)
        query = jnp.concatenate(
            [query[:, g * QDIM : (g + 1) * QDIM] for g in range(group_size)], axis=0
        )
        kcol = pair * 2 * QDIM
        keys = cache_ref[0, :, kcol : kcol + QDIM]
        values = cache_ref[0, :, kcol + QDIM : kcol + 2 * QDIM]
        score_ref[...] = last_dot(query, keys)
        tree_score = last_dot(query, tree_pairs[:, kcol : kcol + QDIM])
        sums = []
        tree_probs = []
        for g in range(group_size):
            rows = slice(g * nodes, (g + 1) * nodes)
            cache_part = jnp.where(valid, score_ref[rows, :], -1e30)
            tree_part = jnp.where(tree_valid, tree_score[rows], -1e30)
            peak = jnp.maximum(
                jnp.max(cache_part, axis=1, keepdims=True),
                jnp.max(tree_part, axis=1, keepdims=True),
            )
            cache_exp = jnp.exp((cache_part - peak) * query_scale)
            tree_exp = jnp.exp((tree_part - peak) * query_scale)
            sums.append(
                jnp.sum(cache_exp, axis=1, keepdims=True)
                + jnp.sum(tree_exp, axis=1, keepdims=True)
            )
            prob_ref[rows, :] = cache_exp.astype(BF16)
            tree_probs.append(tree_exp.astype(BF16))
        result = jnp.dot(prob_ref[...], values, preferred_element_type=F32)
        result = result + jnp.dot(
            jnp.concatenate(tree_probs, axis=0),
            tree_pairs[:, kcol + QDIM : kcol + 2 * QDIM],
            preferred_element_type=F32,
        )
        for g in range(group_size):
            attend_ref[:, first + g * QDIM : first + (g + 1) * QDIM] = (
                result[g * nodes : (g + 1) * nodes] / sums[g]
            ).astype(BF16)

    raw = ordered(step_start, LANES)[:, :head_local] + bias_ref[...]
    step = jnp.maximum(raw, 0.0) + jnp.log1p(jnp.exp(-jnp.abs(raw)))
    cumulative = jnp.dot(
        mask_float,
        -decay_ref[...] * step,
        precision=lax.Precision.HIGHEST,
        preferred_element_type=F32,
    )
    cumulative_t = cumulative.T
    step_t = step.T
    accepted = accepted_ref[0]
    node_sub = lax.broadcasted_iota(jnp.int32, (nodes, head_local), 0)
    lane_of = lax.broadcasted_iota(jnp.int32, (head_local, nodes), 1)
    pick = jnp.sum(jnp.where(node_sub == accepted, cumulative, 0.0), axis=0, keepdims=True)
    node_lanes = lax.broadcasted_iota(jnp.int32, (nodes, nodes), 1)
    mask_pick = jnp.sum(
        jnp.where(node_lanes == accepted, mask_float.T, 0.0), axis=1, keepdims=True
    )
    path = mask_pick * jnp.exp(jnp.minimum(pick - cumulative, 0.0)) * step
    pick_col = jnp.sum(jnp.where(lane_of == accepted, cumulative_t, 0.0), axis=1, keepdims=True)
    keep_ref[...] = jnp.broadcast_to(jnp.exp(pick_col), keep_ref.shape)
    skip_row = skip_ref[...]

    groups = proj_width // (2 * STATE)
    per_group = head_local // groups
    wide = LANES // HEAD_DIM
    low = lax.broadcasted_iota(jnp.int32, (nodes, LANES), 1) < HEAD_DIM
    low_row = lax.broadcasted_iota(jnp.int32, (1, LANES), 1) < HEAD_DIM

    def spread(table, head, rows_low):
        return jnp.where(rows_low, table[:, head : head + 1], table[:, head + 1 : head + 2])

    def pair_row(table, head):
        return jnp.concatenate([table[head : head + 1], table[head + 1 : head + 2]], axis=1)

    for group in range(groups):
        proj = ordered(proj_start + group * 2 * STATE, 2 * STATE).astype(BF16)
        write_rows = proj[:, :STATE]
        read_rows = proj[:, STATE:]
        write_ref[:, group * STATE : (group + 1) * STATE] = write_rows
        inner = last_dot(read_rows, write_rows) * mask_float
        inner = jnp.concatenate([inner] * wide, axis=1)
        state = state_ref[0, group * per_group : (group + 1) * per_group]
        carried = last_dot(read_rows, state.reshape(per_group * HEAD_DIM, STATE))
        for pair in range(per_group // wide):
            head = group * per_group + pair * wide
            lanes = slice(head * HEAD_DIM, head * HEAD_DIM + LANES)
            decay_i = spread(cumulative, head, low)
            decay_j = pair_row(cumulative_t, head)
            step_j = pair_row(step_t, head)
            weight = jnp.exp(jnp.minimum(decay_i - decay_j, 0.0)) * inner * step_j
            weight_ref[:, lanes] = weight.astype(BF16)
            base_ref[:, lanes] = (
                jnp.exp(decay_i) * carried[:, pair * LANES : (pair + 1) * LANES]
            )
            path_ref[:, lanes] = spread(path, head, low)
            skip_out_ref[:, lanes] = spread(skip_row, head, low_row)


def mix(block_refs, reorder, cap_rows, *refs):
    blocks, refs = refs[:block_refs], refs[block_refs:]
    order_ref, weight_ref, base_ref, path_ref, skip_ref = refs[:5]
    mixed_ref, square_ref, weighted_ref = refs[5:]
    nodes, width = base_ref.shape
    order = order_ref[...]
    if reorder:
        slot_total = order.shape[1]
        sub = lax.broadcasted_iota(jnp.int32, (slot_total, slot_total), 0)
        lane = lax.broadcasted_iota(jnp.int32, (slot_total, slot_total), 1)
        move = lax.axis_index("req") * cap_rows
        turn = jnp.where(jnp.bitwise_xor(sub, move) == lane, 1.0, 0.0).astype(BF16)
        order = jnp.dot(order, turn, preferred_element_type=F32).astype(BF16)
    sub = lax.broadcasted_iota(jnp.int32, (2 * nodes, LANES), 0) < nodes
    lane = lax.broadcasted_iota(jnp.int32, (2 * nodes, LANES), 1) < HEAD_DIM
    same = sub == lane
    total = jnp.zeros((nodes, LANES), F32)
    chunk = 4 * LANES
    for start in range(0, width, chunk):
        wide = jnp.dot(order, joined(blocks, start, chunk), preferred_element_type=F32)
        rows = wide.astype(BF16)
        for begin in range(0, chunk, LANES):
            lanes = slice(start + begin, start + begin + LANES)
            one = rows[:, begin : begin + LANES]
            one_wide = wide[:, begin : begin + LANES]
            both = jnp.concatenate([one, one], axis=0)
            both = jnp.where(same, both, jnp.zeros_like(both))
            mixed = jnp.dot(weight_ref[:, lanes], both, preferred_element_type=F32)
            mixed = mixed + base_ref[:, lanes] + skip_ref[:, lanes] * one_wide
            mixed_ref[:, lanes] = mixed
            total = total + mixed * mixed
            weighted_ref[:, lanes] = (path_ref[:, lanes] * one_wide).astype(BF16)
    square_ref[...] = jnp.broadcast_to(jnp.sum(total, axis=1, keepdims=True), square_ref.shape)


def advance(weighted_ref, write_ref, keep_ref, state_ref, out_ref):
    head_local = state_ref.shape[1]
    groups = write_ref.shape[1] // STATE
    per_group = head_local // groups
    for group in range(groups):
        width = per_group * HEAD_DIM
        update = lax.dot_general(
            weighted_ref[:, group * width : (group + 1) * width],
            write_ref[:, group * STATE : (group + 1) * STATE],
            (((0,), (0,)), ((), ())),
            preferred_element_type=F32,
        )
        for index in range(per_group):
            head = group * per_group + index
            out_ref[0, head] = (
                keep_ref[head : head + 1, :] * state_ref[0, head].astype(F32)
                + update[index * HEAD_DIM : (index + 1) * HEAD_DIM]
            ).astype(BF16)


def normalise(total_width, mixed_ref, mine_ref, other_ref, gain_ref, out_ref):
    square = mine_ref[...] + other_ref[...]
    scale = 1.0 / jnp.sqrt(square / total_width + 1e-05)
    width = mixed_ref.shape[1]
    for start in range(0, width, LANES):
        lanes = slice(start, start + LANES)
        out_ref[:, lanes] = (mixed_ref[:, lanes] * scale * gain_ref[:, lanes]).astype(BF16)


def call(body, outs, in_specs=None, scratch=(), name=None):
    def run(*operands):
        specs = in_specs or [pl.BlockSpec(memory_space=pltpu.VMEM)] * len(operands)
        return pl.pallas_call(
            body,
            out_shape=outs,
            in_specs=specs,
            out_specs=tuple(pl.BlockSpec(memory_space=pltpu.VMEM) for _ in outs),
            scratch_shapes=scratch,
            name=name,
            compiler_params=pltpu.CompilerParams(vmem_limit_bytes=50 * 1024 * 1024),
        )(*operands)

    return run


def local(
    draft_input,
    draft_proj,
    draft_step,
    draft_query,
    draft_keyval,
    row_target,
    tree_mask,
    accepted,
    cache_length,
    scan_state,
    cache_keyval,
    decay_rate,
    step_bias,
    skip_gain,
    norm_gain,
):
    shape = jax.ShapeDtypeStruct
    row_count, scan_width = draft_input.shape
    peers = lax.axis_size("req")
    head_shards = lax.axis_size("head")
    cap_rows = max(2, row_count // peers)
    slot_total = peers * cap_rows
    direct = peers <= 16 and peers & (peers - 1) == 0
    head_local = scan_width // HEAD_DIM
    query_width = draft_query.shape[1]
    keyval_width = draft_keyval.shape[1]
    proj_width = draft_proj.shape[1]
    first_width = query_width + keyval_width + proj_width + LANES
    target = row_target.reshape(1, row_count)

    count = peers if direct else 1
    first_blocks = call(
        functools.partial(pack_first, row_count, cap_rows, peers, direct),
        tuple(shape((slot_total // count, first_width), BF16) for _ in range(count)),
        name="pack_first",
    )(target, draft_query, draft_keyval, draft_proj, draft_step)
    second = call(
        functools.partial(pack_second, row_count, cap_rows, peers, False),
        (shape((slot_total, scan_width), BF16),),
        name="pack_second",
    )(target, draft_input)[0]

    def exchange(blocks):
        if direct:
            arrived = [blocks[0]]
            for step in range(1, peers):
                pairs = [(index, index ^ step) for index in range(peers)]
                arrived.append(lax.ppermute(blocks[step], "req", pairs))
            return arrived
        return [all_to_all(blocks[0])]

    def all_to_all(rows):
        split = rows.reshape(peers, cap_rows, -1)
        moved = lax.all_to_all(split, "req", split_axis=0, concat_axis=0, tiled=True)
        return moved.reshape(slot_total, -1)

    first_arrived = exchange(first_blocks)
    second_arrived = [all_to_all(second)]

    scalar = pl.BlockSpec(memory_space=pltpu.SMEM)
    vector = pl.BlockSpec(memory_space=pltpu.VMEM)
    pair_heads = keyval_width // (2 * QDIM)
    score_rows = NODES * (query_width // QDIM // pair_heads)
    cache_count = cache_keyval.shape[1]
    groups = proj_width // (2 * STATE)
    attend_out, weight, base, path, keep, write, order, skip_wide = call(
        functools.partial(
            middle,
            len(first_arrived),
            False,
            cap_rows,
            (query_width, keyval_width, proj_width, head_local),
        ),
        (
            shape((row_count, query_width), BF16),
            shape((NODES, head_local * NODES), BF16),
            shape((NODES, scan_width), F32),
            shape((NODES, scan_width), F32),
            shape((head_local, LANES), F32),
            shape((NODES, groups * STATE), BF16),
            shape((NODES, slot_total), BF16),
            shape((1, scan_width), F32),
        ),
        in_specs=[vector] * len(first_arrived) + [scalar] * 2 + [vector] * 6,
        scratch=[
            pltpu.VMEM((score_rows, cache_count), F32),
            pltpu.VMEM((score_rows, cache_count), BF16),
        ],
        name="middle",
    )(
        *first_arrived,
        accepted,
        cache_length,
        tree_mask,
        scan_state,
        cache_keyval,
        decay_rate.reshape(1, head_local),
        step_bias.reshape(1, head_local),
        skip_gain.reshape(1, head_local),
    )

    mixed, square, weighted = call(
        functools.partial(mix, len(second_arrived), direct, cap_rows),
        (
            shape((NODES, scan_width), F32),
            shape((NODES, LANES), F32),
            shape((NODES, scan_width), BF16),
        ),
        name="mix",
    )(*second_arrived, order, weight, base, path, skip_wide)
    swap = [(index, (index + 1) % head_shards) for index in range(head_shards)]
    other = lax.ppermute(square, "head", swap)
    new_state = call(
        advance, (shape(scan_state.shape, BF16),), name="advance"
    )(weighted, write, keep, scan_state)[0]
    mixer_out = call(
        functools.partial(normalise, head_shards * scan_width),
        (shape((row_count, scan_width), BF16),),
        name="normalise",
    )(mixed, square, other, norm_gain.reshape(1, scan_width))[0]
    return (mixer_out, attend_out, new_state)


def solution(mesh):
    assert mesh.shape["head"] == 2
    rows = P(("grp", "req"), "head")
    return jax.shard_map(
        local,
        mesh=mesh,
        in_specs=(
            rows,
            rows,
            rows,
            rows,
            rows,
            P(("grp", "req")),
            P(("grp", "req"), None, None),
            P(("grp", "req")),
            P(("grp", "req")),
            P(("grp", "req"), "head", None, None),
            P(("grp", "req"), None, "head"),
            P("head"),
            P("head"),
            P("head"),
            P("head"),
        ),
        out_specs=(rows, rows, P(("grp", "req"), "head", None, None)),
        check_vma=False,
    )
```

```python
import functools

import jax
import jax.numpy as jnp
from jax import lax
from jax.experimental import pallas as pl
from jax.experimental.pallas import tpu as pltpu
from jax.sharding import PartitionSpec as P


HEAD_DIM = 64
STATE = 128
QDIM = 128
NODES = 64
LANES = 128
F32 = jnp.float32
BF16 = jnp.bfloat16


def last_dot(left, right):
    return lax.dot_general(left, right, (((1,), (1,)), ((), ())), preferred_element_type=F32)


def row_to_column(row):
    size = row.shape[1]
    sub = lax.broadcasted_iota(jnp.int32, (size, size), 0)
    lane = lax.broadcasted_iota(jnp.int32, (size, size), 1)
    spread = jnp.broadcast_to(row, (size, size))
    return jnp.sum(jnp.where(sub == lane, spread, jnp.zeros_like(spread)), axis=1, keepdims=True)


def slot_one_hot(target, row_count, cap_rows, slot_total, me):
    shift = row_count.bit_length() - 1
    peer = lax.shift_right_logical(target, jnp.full_like(target, shift))
    local = target - peer * row_count
    peer_f = peer.astype(F32)
    peer_col = row_to_column(peer_f)
    size = row_count
    sub = lax.broadcasted_iota(jnp.int32, (size, size), 0)
    lane = lax.broadcasted_iota(jnp.int32, (size, size), 1)
    same = jnp.logical_and(peer_col == peer_f, sub < lane)
    rank = jnp.sum(jnp.where(same, 1.0, 0.0), axis=0, keepdims=True).astype(jnp.int32)
    block = peer if me is None else jnp.bitwise_xor(peer, jnp.full_like(peer, me))
    slot = block * cap_rows + rank
    slots = lax.broadcasted_iota(jnp.int32, (slot_total, size), 0)
    return jnp.where(slots == slot, 1.0, 0.0).astype(BF16), local


def pack(sizes, xor_blocks, layout, *refs):
    row_count, cap_rows, block_count = sizes
    target_hbm, sources, refs = refs[0], refs[1:6], refs[6:]
    outs, held_target, held, sems = refs[:-7], refs[-7], refs[-6:-1], refs[-1]
    target_copy = pltpu.make_async_copy(target_hbm, held_target, sems.at[5])
    target_copy.start()
    copies = [
        pltpu.make_async_copy(source, buffer, sems.at[index])
        for index, (source, buffer) in enumerate(zip(sources, held))
    ]
    for copy in copies:
        copy.start()
    me = lax.axis_index("req") if xor_blocks else None
    slot_total = block_count * cap_rows
    target_copy.wait()
    chosen, local = slot_one_hot(held_target[...], row_count, cap_rows, slot_total, me)
    column = 0
    for index, buffer in enumerate(held):
        copies[index].wait()
        part = buffer[...]
        width = part.shape[1]
        if index == len(held) - 1:
            local_col = row_to_column((local + 1).astype(F32))
            labels = jnp.broadcast_to(local_col, (row_count, LANES - width)).astype(BF16)
            part = jnp.concatenate([part, labels], axis=1)
            width = LANES
        moved = jnp.dot(chosen, part, preferred_element_type=F32).astype(BF16)
        for out_ref, (first_block, blocks, start) in zip(outs, layout):
            if start <= column < start + out_ref.shape[1]:
                rows = slice(first_block * cap_rows, (first_block + blocks) * cap_rows)
                out_ref[:, column - start : column - start + width] = moved[rows]
        column += width


def joined(views, start, width):
    parts = [ref[:, start - offset : start - offset + width] for ref, offset in views]
    return parts[0] if len(parts) == 1 else jnp.concatenate(parts, axis=0)


def middle(offsets, sizes, *refs):
    query_width, keyval_width, proj_width, head_local, query_start = sizes
    blocks, refs = tuple(zip(refs, offsets)), refs[len(offsets) :]
    scalar_ref, mask_hbm, decay_hbm, bias_hbm, skip_hbm, state_hbm, cache_hbm, gain_hbm = refs[:8]
    attend_hbm, weight_ref, base_ref, path_ref, kept_ref = refs[8:13]
    write_ref, order_ref, skip_out_ref, gain_ref = refs[13:17]
    mask_ref, decay_ref, bias_ref, skip_ref, state_ref, cache_ref = refs[17:23]
    attend_ref, score_ref, prob_ref, sems, out_sems = refs[23:]
    sources = (mask_hbm, decay_hbm, bias_hbm, skip_hbm, state_hbm, cache_hbm, gain_hbm)
    targets = (mask_ref, decay_ref, bias_ref, skip_ref, state_ref, cache_ref, gain_ref)
    loads = [
        pltpu.make_async_copy(source, held, sems.at[index])
        for index, (source, held) in enumerate(zip(sources, targets))
    ]
    for load in loads:
        load.start()
    nodes = mask_ref.shape[1]
    kv_start = query_start + query_width
    proj_start = kv_start + keyval_width
    step_start = proj_start + proj_width
    tail = joined(blocks, step_start, LANES)
    label_lane = tail[:, LANES - nodes :].astype(F32)
    slot_total = tail.shape[0]
    node_lane = lax.broadcasted_iota(jnp.int32, (slot_total, nodes), 1).astype(F32) + 1.0
    order = jnp.where(label_lane == node_lane, 1.0, 0.0).T.astype(BF16)
    order_ref[...] = order

    def ordered(start, width):
        return jnp.dot(order, joined(blocks, start, width), preferred_element_type=F32)

    for load in loads[:4]:
        load.wait()
    mask_float = mask_ref[0].astype(F32)
    raw = ordered(step_start, LANES)[:, :head_local] + bias_ref[...]
    step = jnp.maximum(raw, 0.0) + jnp.log1p(jnp.exp(-jnp.abs(raw)))
    cumulative = jnp.dot(
        mask_float,
        -decay_ref[...] * step,
        precision=lax.Precision.HIGHEST,
        preferred_element_type=F32,
    )
    cumulative_t = cumulative.T
    step_t = step.T
    accepted = scalar_ref[0:1, 0:1]
    node_sub = lax.broadcasted_iota(jnp.int32, (nodes, head_local), 0)
    lane_of = lax.broadcasted_iota(jnp.int32, (head_local, nodes), 1)
    pick = jnp.sum(jnp.where(node_sub == accepted, cumulative, 0.0), axis=0, keepdims=True)
    node_lanes = lax.broadcasted_iota(jnp.int32, (nodes, nodes), 1)
    mask_pick = jnp.sum(
        jnp.where(node_lanes == accepted, mask_float.T, 0.0), axis=1, keepdims=True
    )
    path = mask_pick * jnp.exp(jnp.minimum(pick - cumulative, 0.0)) * step
    pick_col = jnp.sum(jnp.where(lane_of == accepted, cumulative_t, 0.0), axis=1, keepdims=True)
    keep = jnp.broadcast_to(jnp.exp(pick_col), (head_local, LANES))
    skip_row = skip_ref[...]

    groups = proj_width // (2 * STATE)
    per_group = head_local // groups
    wide = LANES // HEAD_DIM
    low = lax.broadcasted_iota(jnp.int32, (nodes, LANES), 1) < HEAD_DIM
    low_row = lax.broadcasted_iota(jnp.int32, (1, LANES), 1) < HEAD_DIM

    def spread(table, head, rows_low):
        return jnp.where(rows_low, table[:, head : head + 1], table[:, head + 1 : head + 2])

    def pair_row(table, head):
        return jnp.concatenate([table[head : head + 1], table[head + 1 : head + 2]], axis=1)

    loads[4].wait()
    for group in range(groups):
        proj = ordered(proj_start + group * 2 * STATE, 2 * STATE).astype(BF16)
        write_rows = proj[:, :STATE]
        read_rows = proj[:, STATE:]
        write_ref[:, group * STATE : (group + 1) * STATE] = write_rows
        inner = last_dot(read_rows, write_rows) * mask_float
        inner = jnp.concatenate([inner] * wide, axis=1)
        state = state_ref[0, group * per_group : (group + 1) * per_group]
        carried = last_dot(read_rows, state.reshape(per_group * HEAD_DIM, STATE))
        for pair in range(per_group // wide):
            head = group * per_group + pair * wide
            lanes = slice(head * HEAD_DIM, head * HEAD_DIM + LANES)
            decay_i = spread(cumulative, head, low)
            decay_j = pair_row(cumulative_t, head)
            step_j = pair_row(step_t, head)
            weight = jnp.exp(jnp.minimum(decay_i - decay_j, 0.0)) * inner * step_j
            weight_ref[:, lanes] = weight.astype(BF16)
            base_ref[:, lanes] = (
                jnp.exp(decay_i) * carried[:, pair * LANES : (pair + 1) * LANES]
            )
            path_ref[:, lanes] = spread(path, head, low)
            skip_out_ref[:, lanes] = spread(skip_row, head, low_row)
    for head in range(head_local):
        kept_ref[head] = keep[head : head + 1, :] * state_ref[0, head].astype(F32)

    pair_heads = keyval_width // (2 * QDIM)
    group_size = query_width // QDIM // pair_heads
    cache_count = cache_ref.shape[1]
    query_scale = QDIM ** (-0.5)
    length = scalar_ref[1:2, 0:1]
    valid = lax.broadcasted_iota(jnp.int32, (1, cache_count), 1) < length
    tree_valid = mask_float > 0.0
    tree_pairs = ordered(kv_start, keyval_width).astype(BF16)
    loads[5].wait()
    stores = []
    for pair in range(pair_heads):
        first = pair * group_size * QDIM
        query = ordered(query_start + first, group_size * QDIM).astype(BF16)
        query = jnp.concatenate(
            [query[:, g * QDIM : (g + 1) * QDIM] for g in range(group_size)], axis=0
        )
        kcol = pair * 2 * QDIM
        keys = cache_ref[0, :, kcol : kcol + QDIM]
        values = cache_ref[0, :, kcol + QDIM : kcol + 2 * QDIM]
        score_ref[...] = last_dot(query, keys)
        tree_score = last_dot(query, tree_pairs[:, kcol : kcol + QDIM])
        sums = []
        tree_probs = []
        for g in range(group_size):
            rows = slice(g * nodes, (g + 1) * nodes)
            cache_part = jnp.where(valid, score_ref[rows, :], -1e30)
            tree_part = jnp.where(tree_valid, tree_score[rows], -1e30)
            peak = jnp.maximum(
                jnp.max(cache_part, axis=1, keepdims=True),
                jnp.max(tree_part, axis=1, keepdims=True),
            )
            cache_exp = jnp.exp((cache_part - peak) * query_scale)
            tree_exp = jnp.exp((tree_part - peak) * query_scale)
            sums.append(
                jnp.sum(cache_exp, axis=1, keepdims=True)
                + jnp.sum(tree_exp, axis=1, keepdims=True)
            )
            prob_ref[rows, :] = cache_exp.astype(BF16)
            tree_probs.append(tree_exp.astype(BF16))
        result = jnp.dot(prob_ref[...], values, preferred_element_type=F32)
        result = result + jnp.dot(
            jnp.concatenate(tree_probs, axis=0),
            tree_pairs[:, kcol + QDIM : kcol + 2 * QDIM],
            preferred_element_type=F32,
        )
        for g in range(group_size):
            attend_ref[:, first + g * QDIM : first + (g + 1) * QDIM] = (
                result[g * nodes : (g + 1) * nodes] / sums[g]
            ).astype(BF16)
        lanes = pl.ds(first, group_size * QDIM)
        stores.append(
            pltpu.make_async_copy(
                attend_ref.at[:, lanes], attend_hbm.at[:, lanes], out_sems.at[pair]
            )
        )
        stores[-1].start()
    loads[6].wait()
    for store in stores:
        store.wait()


def mix(offsets, *refs):
    blocks, refs = tuple(zip(refs, offsets)), refs[len(offsets) :]
    order_ref, weight_ref, base_ref, path_ref, skip_ref = refs[:5]
    mixed_ref, square_ref, weighted_ref = refs[5:]
    nodes, width = mixed_ref.shape
    order = order_ref[...]
    sub = lax.broadcasted_iota(jnp.int32, (2 * nodes, LANES), 0) < nodes
    lane = lax.broadcasted_iota(jnp.int32, (2 * nodes, LANES), 1) < HEAD_DIM
    same = sub == lane
    total = jnp.zeros((nodes, LANES), F32)
    chunk = 4 * LANES
    for start in range(0, width, chunk):
        wide = jnp.dot(order, joined(blocks, start, chunk), preferred_element_type=F32)
        rows = wide.astype(BF16)
        for begin in range(0, chunk, LANES):
            lanes = slice(start + begin, start + begin + LANES)
            one = rows[:, begin : begin + LANES]
            one_wide = wide[:, begin : begin + LANES]
            both = jnp.concatenate([one, one], axis=0)
            both = jnp.where(same, both, jnp.zeros_like(both))
            mixed = jnp.dot(weight_ref[:, lanes], both, preferred_element_type=F32)
            mixed = mixed + base_ref[:, lanes] + skip_ref[:, lanes] * one_wide
            mixed_ref[:, lanes] = mixed
            total = total + mixed * mixed
            weighted_ref[:, lanes] = (path_ref[:, lanes] * one_wide).astype(BF16)
    square_ref[...] = jnp.broadcast_to(jnp.sum(total, axis=1, keepdims=True), square_ref.shape)


def advance(weighted_ref, write_ref, kept_ref, out_hbm, out_ref, sems):
    head_local = kept_ref.shape[0]
    groups = write_ref.shape[1] // STATE
    per_group = head_local // groups
    width = per_group * HEAD_DIM
    stores = []
    for group in range(groups):
        update = lax.dot_general(
            weighted_ref[:, group * width : (group + 1) * width],
            write_ref[:, group * STATE : (group + 1) * STATE],
            (((0,), (0,)), ((), ())),
            preferred_element_type=F32,
        )
        for index in range(per_group):
            head = group * per_group + index
            out_ref[0, head] = (
                kept_ref[head] + update[index * HEAD_DIM : (index + 1) * HEAD_DIM]
            ).astype(BF16)
        heads = pl.ds(group * per_group, per_group)
        stores.append(
            pltpu.make_async_copy(out_ref.at[:, heads], out_hbm.at[:, heads], sems.at[group])
        )
        stores[-1].start()
    for store in stores:
        store.wait()


def normalise(total_width, mixed_ref, mine_ref, other_ref, gain_ref, out_hbm, out_ref, sems):
    square = mine_ref[...] + other_ref[...]
    scale = 1.0 / jnp.sqrt(square / total_width + 1e-05)
    chunks = sems.shape[0]
    width = out_ref.shape[1] // chunks
    stores = []
    for chunk in range(chunks):
        for start in range(chunk * width, (chunk + 1) * width, LANES):
            lanes = slice(start, start + LANES)
            out_ref[:, lanes] = (mixed_ref[:, lanes] * scale * gain_ref[:, lanes]).astype(BF16)
        view = pl.ds(chunk * width, width)
        stores.append(
            pltpu.make_async_copy(out_ref.at[:, view], out_hbm.at[:, view], sems.at[chunk])
        )
        stores[-1].start()
    for store in stores:
        store.wait()


SPACES = {"h": pltpu.HBM, "v": pltpu.VMEM, "s": pltpu.SMEM}


def call(body, ins, outs, scratch=(), mebibytes=8):
    def run(*operands):
        placed = [
            operand if space == "s" else pltpu.with_memory_space_constraint(operand, SPACES[space])
            for space, operand in zip(ins, operands, strict=True)
        ]
        return pl.pallas_call(
            body,
            out_shape=tuple(SPACES[space](dims, kind) for space, dims, kind in outs),
            in_specs=[pl.BlockSpec(memory_space=SPACES[space]) for space in ins],
            out_specs=tuple(pl.BlockSpec(memory_space=SPACES[out[0]]) for out in outs),
            scratch_shapes=scratch,
            compiler_params=pltpu.CompilerParams(vmem_limit_bytes=mebibytes * 1024 * 1024),
        )(*placed)

    return run


def local(
    draft_input,
    draft_proj,
    draft_step,
    draft_query,
    draft_keyval,
    row_target,
    tree_mask,
    accepted,
    cache_length,
    scan_state,
    cache_keyval,
    decay_rate,
    step_bias,
    skip_gain,
    norm_gain,
):
    row_count, scan_width = draft_input.shape
    peers = lax.axis_size("req")
    head_shards = lax.axis_size("head")
    cap_rows = max(2, row_count // peers)
    slot_total = peers * cap_rows
    direct = peers <= 16 and peers & (peers - 1) == 0
    head_local = scan_width // HEAD_DIM
    query_width = draft_query.shape[1]
    keyval_width = draft_keyval.shape[1]
    proj_width = draft_proj.shape[1]
    groups = proj_width // (2 * STATE)
    all_width = scan_width + query_width + keyval_width + proj_width + LANES
    near = peers // 2 if direct else 0
    if direct:
        layout = [(block, 1, 0) for block in range(near)]
        layout += [(block, 1, scan_width) for block in range(near, peers)]
        layout += [(block, 1, 0) for block in range(near, peers)]
        widths = [all_width] * near + [all_width - scan_width] * (peers - near)
        widths += [scan_width] * (peers - near)
    else:
        layout, widths = [(0, peers, 0)], [all_width]
    sources = (draft_input, draft_query, draft_keyval, draft_proj, draft_step)
    packed = call(
        functools.partial(pack, (row_count, cap_rows, peers), direct, layout),
        "h" * 6,
        tuple(
            ("v", (blocks * cap_rows, width), BF16)
            for (_, blocks, _), width in zip(layout, widths)
        ),
        scratch=[pltpu.VMEM((1, row_count), jnp.int32)]
        + [pltpu.VMEM(source.shape, BF16) for source in sources]
        + [pltpu.SemaphoreType.DMA((6,))],
    )(row_target.reshape(1, row_count), *sources)

    def moved(block, step):
        pairs = [(index, index ^ step) for index in range(peers)]
        return lax.ppermute(block, "req", pairs)

    if direct:
        whole = [packed[0]] + [moved(packed[step], step) for step in range(1, near)]
        far = range(near, peers)
        firsts = [moved(packed[step], step) for step in far]
        seconds = [moved(packed[step + peers - near], step) for step in far]
        first_blocks, first_offsets = whole + firsts, [0] * near + [scan_width] * len(far)
        second_blocks, second_offsets = whole + seconds, [0] * peers
    else:
        split = packed[0].reshape(peers, cap_rows, all_width)
        arrived = lax.all_to_all(split, "req", split_axis=0, concat_axis=0, tiled=True)
        first_blocks = second_blocks = [arrived.reshape(slot_total, all_width)]
        first_offsets = second_offsets = [0]

    scalars = jnp.broadcast_to(jnp.stack([accepted, cache_length]), (2, LANES))
    pair_heads = keyval_width // (2 * QDIM)
    score_rows = NODES * (query_width // QDIM // pair_heads)
    cache_count = cache_keyval.shape[1]
    attend_out, weight, base, path, kept, write, order, skip_wide, gain = call(
        functools.partial(
            middle,
            first_offsets,
            (query_width, keyval_width, proj_width, head_local, scan_width),
        ),
        "v" * (len(first_blocks) + 1) + "h" * 7,
        (
            ("h", (row_count, query_width), BF16),
            ("v", (NODES, head_local * NODES), BF16),
            ("v", (NODES, scan_width), F32),
            ("v", (NODES, scan_width), F32),
            ("v", (head_local, HEAD_DIM, STATE), F32),
            ("v", (NODES, groups * STATE), BF16),
            ("v", (NODES, slot_total), BF16),
            ("v", (1, scan_width), F32),
            ("v", (1, scan_width), F32),
        ),
        scratch=[
            pltpu.VMEM(tree_mask.shape, jnp.int32),
            pltpu.VMEM((1, head_local), F32),
            pltpu.VMEM((1, head_local), F32),
            pltpu.VMEM((1, head_local), F32),
            pltpu.VMEM(scan_state.shape, BF16),
            pltpu.VMEM(cache_keyval.shape, BF16),
            pltpu.VMEM((row_count, query_width), BF16),
            pltpu.VMEM((score_rows, cache_count), F32),
            pltpu.VMEM((score_rows, cache_count), BF16),
            pltpu.SemaphoreType.DMA((7,)),
            pltpu.SemaphoreType.DMA((pair_heads,)),
        ],
        mebibytes=24,
    )(
        *first_blocks,
        scalars,
        tree_mask,
        decay_rate.reshape(1, head_local),
        step_bias.reshape(1, head_local),
        skip_gain.reshape(1, head_local),
        scan_state,
        cache_keyval,
        norm_gain.reshape(1, scan_width),
    )

    mixed, square, weighted = call(
        functools.partial(mix, second_offsets),
        "v" * (len(second_blocks) + 5),
        (
            ("v", (NODES, scan_width), F32),
            ("v", (NODES, LANES), F32),
            ("v", (NODES, scan_width), BF16),
        ),
    )(*second_blocks, order, weight, base, path, skip_wide)
    swap = [(index, (index + 1) % head_shards) for index in range(head_shards)]
    other = lax.ppermute(square, "head", swap)
    new_state = call(
        advance,
        "v" * 3,
        (("h", scan_state.shape, BF16),),
        scratch=[pltpu.VMEM(scan_state.shape, BF16), pltpu.SemaphoreType.DMA((groups,))],
    )(weighted, write, kept)[0]
    mixer_out = call(
        functools.partial(normalise, head_shards * scan_width),
        "v" * 4,
        (("h", (row_count, scan_width), BF16),),
        scratch=[pltpu.VMEM((row_count, scan_width), BF16), pltpu.SemaphoreType.DMA((groups,))],
    )(mixed, square, other, gain)[0]
    return (mixer_out, attend_out, new_state)


def solution(mesh):
    assert mesh.shape["head"] == 2
    rows = P(("grp", "req"), "head")

    return jax.shard_map(
        local,
        mesh=mesh,
        in_specs=(
            rows,
            rows,
            rows,
            rows,
            rows,
            P(("grp", "req")),
            P(("grp", "req"), None, None),
            P(("grp", "req")),
            P(("grp", "req")),
            P(("grp", "req"), "head", None, None),
            P(("grp", "req"), None, "head"),
            P("head"),
            P("head"),
            P("head"),
            P("head"),
        ),
        out_specs=(rows, rows, P(("grp", "req"), "head", None, None)),
        check_vma=False,
    )
```

```python
import functools

import jax
import jax.numpy as jnp
from jax import lax
from jax.experimental import pallas as pl
from jax.experimental.pallas import tpu as pltpu
from jax.sharding import PartitionSpec as P


HEAD_DIM = 64
STATE = 128
QDIM = 128
NODES = 64
LANES = 128
LOG2E = 1.4426950408889634
FAR = -1e30
EARLY = 0.0
F32 = jnp.float32
BF16 = jnp.bfloat16


def last_dot(left, right):
    return lax.dot_general(left, right, (((1,), (1,)), ((), ())), preferred_element_type=F32)


def row_to_column(row):
    size = row.shape[1]
    sub = lax.broadcasted_iota(jnp.int32, (size, size), 0)
    lane = lax.broadcasted_iota(jnp.int32, (size, size), 1)
    spread = jnp.broadcast_to(row, (size, size))
    return jnp.sum(jnp.where(sub == lane, spread, jnp.zeros_like(spread)), axis=1, keepdims=True)


def slot_one_hot(target, row_count, cap_rows, slot_total, me):
    shift = row_count.bit_length() - 1
    peer = lax.shift_right_logical(target, jnp.full_like(target, shift))
    local = target - peer * row_count
    peer_f = peer.astype(F32)
    peer_col = row_to_column(peer_f)
    size = row_count
    sub = lax.broadcasted_iota(jnp.int32, (size, size), 0)
    lane = lax.broadcasted_iota(jnp.int32, (size, size), 1)
    same = jnp.logical_and(peer_col == peer_f, sub < lane)
    rank = jnp.sum(jnp.where(same, 1.0, 0.0), axis=0, keepdims=True).astype(jnp.int32)
    block = peer if me is None else jnp.bitwise_xor(peer, jnp.full_like(peer, me))
    slot = block * cap_rows + rank
    slots = lax.broadcasted_iota(jnp.int32, (slot_total, size), 0)
    return jnp.where(slots == slot, 1.0, 0.0).astype(BF16), local


def pack(sizes, xor_blocks, layout, *refs):
    row_count, cap_rows, block_count = sizes
    target_hbm, sources, refs = refs[0], refs[1:6], refs[6:]
    outs, held_target, held, sems = refs[:-7], refs[-7], refs[-6:-1], refs[-1]
    target_copy = pltpu.make_async_copy(target_hbm, held_target, sems.at[5])
    target_copy.start()
    copies = [
        pltpu.make_async_copy(source, buffer, sems.at[index])
        for index, (source, buffer) in enumerate(zip(sources, held))
    ]
    for copy in copies:
        copy.start()
    me = lax.axis_index("req") if xor_blocks else None
    slot_total = block_count * cap_rows
    target_copy.wait()
    chosen, local = slot_one_hot(held_target[...], row_count, cap_rows, slot_total, me)
    column = 0
    for index, buffer in enumerate(held):
        copies[index].wait()
        part = buffer[...]
        if index == len(held) - 1:
            local_col = row_to_column((local + 1).astype(F32))
            labels = jnp.broadcast_to(local_col, (row_count, LANES - part.shape[1])).astype(BF16)
            part = jnp.concatenate([part, labels], axis=1)
        for begin in range(0, part.shape[1], 4 * LANES):
            piece = part[:, begin : begin + 4 * LANES]
            width = piece.shape[1]
            moved = jnp.dot(chosen, piece, preferred_element_type=F32).astype(BF16)
            for out_ref, pieces in zip(outs, layout):
                for first_block, blocks, start, end, at in pieces:
                    if start <= column < end:
                        rows = slice(first_block * cap_rows, (first_block + blocks) * cap_rows)
                        place = column - start + at
                        out_ref[:, place : place + width] = moved[rows]
            column += width


def forward(own_refs, arrived_ref, out_refs):
    width = own_refs[0].shape[1]
    for index, (own_ref, out_ref) in enumerate(zip(own_refs, out_refs)):
        out_ref[:, :width] = own_ref[...]
        out_ref[:, width:] = arrived_ref[:, (index + 1) * width : (index + 2) * width]


def joined(views, start, width):
    parts = [ref[:, start - offset : start - offset + width] for ref, offset in views]
    return parts[0] if len(parts) == 1 else jnp.concatenate(parts, axis=0)


def middle(offsets, sizes, *refs):
    query_width, keyval_width, proj_width, head_local, query_start = sizes
    blocks, refs = tuple(zip(refs, offsets)), refs[len(offsets) :]
    scalar_ref, mask_hbm, decay_hbm, bias_hbm, skip_hbm, state_hbm, cache_hbm, gain_hbm = refs[:8]
    attend_ref, weight_ref, base_ref, path_ref, kept_ref = refs[8:13]
    write_ref, order_ref, skip_out_ref, gain_ref = refs[13:17]
    mask_ref, decay_ref, bias_ref, skip_ref, state_ref, keys_ref, values_ref = refs[17:24]
    score_ref, prob_ref, rows_ref, sems = refs[24:]
    pair_heads = keyval_width // (2 * QDIM)
    cache_count = cache_hbm.shape[1]
    sources = [mask_hbm, decay_hbm, bias_hbm, skip_hbm, state_hbm, gain_hbm]
    targets = [mask_ref, decay_ref, bias_ref, skip_ref, state_ref, gain_ref]
    for pair in range(pair_heads):
        for part, held in enumerate((keys_ref, values_ref)):
            sources.append(cache_hbm.at[0, :, pl.ds((2 * pair + part) * QDIM, QDIM)])
            targets.append(held.at[pair, pl.ds(0, cache_count), pl.ds(0, QDIM)])
    loads = [
        pltpu.make_async_copy(source, held, sems.at[index])
        for index, (source, held) in enumerate(zip(sources, targets))
    ]
    for load in loads:
        load.start()
    nodes = mask_ref.shape[1]
    kv_start = query_start + query_width
    proj_start = kv_start + keyval_width
    step_start = proj_start + proj_width
    tail = joined(blocks, step_start, LANES)
    label_lane = tail[:, LANES - nodes :].astype(F32)
    slot_total = tail.shape[0]
    node_lane = lax.broadcasted_iota(jnp.int32, (slot_total, nodes), 1).astype(F32) + 1.0
    order = jnp.where(label_lane == node_lane, 1.0, 0.0).T.astype(BF16)
    order_ref[...] = order

    def ordered(start, width):
        return jnp.dot(order, joined(blocks, start, width), preferred_element_type=F32)

    length = scalar_ref[0:1, 1:2]
    key_block = 128
    for start in range(0, cache_count, key_block):
        position = lax.broadcasted_iota(jnp.int32, (key_block, LANES), 0) + start
        bias = jnp.where(position < length, 0.0, FAR).astype(BF16)
        for pair in range(pair_heads):
            keys_ref[pair, start : start + key_block, QDIM:] = bias
    for pair in range(pair_heads):
        values_ref[pair, :, QDIM:] = jnp.ones((values_ref.shape[1], LANES), BF16)

    for load in loads[:4]:
        load.wait()
    mask_float = mask_ref[0].astype(F32)
    raw = ordered(step_start, LANES)[:, :head_local] + bias_ref[...]
    step = jnp.maximum(raw, 0.0) + jnp.log1p(jnp.exp(-jnp.abs(raw)))
    cumulative = jnp.dot(
        mask_float,
        (-LOG2E * decay_ref[...]) * step,
        precision=lax.Precision.HIGHEST,
        preferred_element_type=F32,
    )
    cumulative_t = cumulative.T
    step_t = step.T
    accepted = scalar_ref[0:1, 0:1]
    node_sub = lax.broadcasted_iota(jnp.int32, (nodes, head_local), 0)
    lane_of = lax.broadcasted_iota(jnp.int32, (head_local, nodes), 1)
    pick = jnp.sum(jnp.where(node_sub == accepted, cumulative, 0.0), axis=0, keepdims=True)
    node_lanes = lax.broadcasted_iota(jnp.int32, (nodes, nodes), 1)
    mask_t = mask_float.T
    mask_pick = jnp.sum(jnp.where(node_lanes == accepted, mask_t, 0.0), axis=1, keepdims=True)
    path = mask_pick * jnp.exp2(jnp.minimum(pick - cumulative, 0.0)) * step
    pick_col = jnp.sum(jnp.where(lane_of == accepted, cumulative_t, 0.0), axis=1, keepdims=True)
    keep = jnp.broadcast_to(jnp.exp2(pick_col), (head_local, LANES))

    groups = proj_width // (2 * STATE)
    per_group = head_local // groups
    wide = LANES // HEAD_DIM
    pairs = head_local // wide
    low = lax.broadcasted_iota(jnp.int32, (pairs, LANES), 1) < HEAD_DIM
    rows_ref[0] = jnp.concatenate([cumulative_t] * wide, axis=1)
    rows_ref[1] = jnp.concatenate([step_t] * wide, axis=1)

    def pair_rows(index):
        even = rows_ref[index, pl.ds(0, pairs, stride=2), :]
        odd = rows_ref[index, pl.ds(1, pairs, stride=2), :]
        return jnp.where(low, even, odd)

    decay_pairs, step_pairs = pair_rows(0), pair_rows(1)
    columns = jnp.concatenate([cumulative, path], axis=1)
    skip_columns = jnp.broadcast_to(
        jnp.concatenate([skip_ref[...]] * wide, axis=1), (8, LANES)
    )
    half = lax.broadcasted_iota(jnp.int32, (nodes, LANES), 1) // HEAD_DIM

    def spread(table, column):
        index = half[: table.shape[0]] + column
        return jnp.take_along_axis(table, index, axis=1, mode="promise_in_bounds")

    loads[4].wait()
    for group in range(groups):
        proj = ordered(proj_start + group * 2 * STATE, 2 * STATE).astype(BF16)
        write_rows = proj[:, :STATE]
        read_rows = proj[:, STATE:]
        write_ref[:, group * STATE : (group + 1) * STATE] = write_rows
        inner = last_dot(read_rows, write_rows) * mask_float
        inner = jnp.concatenate([inner] * wide, axis=1)
        for pair in range(per_group // wide):
            head = group * per_group + pair * wide
            lanes = slice(head * HEAD_DIM, head * HEAD_DIM + LANES)
            row = slice(head // wide, head // wide + 1)
            state = state_ref[0, head : head + wide].reshape(wide * HEAD_DIM, STATE)
            carried = last_dot(read_rows, state)
            decay_i = spread(columns, head)
            weight = jnp.exp2(jnp.minimum(decay_i - decay_pairs[row], 0.0))
            weight_ref[:, lanes] = (weight * inner * step_pairs[row]).astype(BF16)
            base_ref[:, lanes] = jnp.exp2(decay_i) * carried
            path_ref[:, lanes] = spread(columns, head_local + head)
            skip_out_ref[:, lanes] = spread(skip_columns, head)[0:1]
            for index in range(head, head + wide):
                kept_ref[index] = keep[index : index + 1, :] * state_ref[0, index].astype(F32)

    group_size = query_width // QDIM // pair_heads
    scale = QDIM ** (-0.5) * LOG2E
    tree_pairs = ordered(kv_start, keyval_width).astype(BF16)
    none = jnp.zeros((keys_ref.shape[1] - cache_count - nodes, QDIM), BF16)
    tree_bias = ((1.0 - mask_t) * FAR).astype(BF16)
    tree_bias = jnp.concatenate([tree_bias, jnp.zeros_like(tree_bias)], axis=1)
    sub = lax.broadcasted_iota(jnp.int32, (nodes, LANES), 0)
    lane = lax.broadcasted_iota(jnp.int32, (nodes, LANES), 1)
    own_node = jnp.where(sub == lane, 1.0, 0.0).astype(BF16)
    tree_end = cache_count + nodes
    for pair in range(pair_heads):
        kcol = pair * 2 * QDIM
        keys_ref[pair, cache_count:tree_end, :QDIM] = tree_pairs[:, kcol : kcol + QDIM]
        keys_ref[pair, cache_count:tree_end, QDIM:] = tree_bias
        keys_ref[pair, tree_end:, :QDIM] = none
        keys_ref[pair, tree_end:, QDIM:] = jnp.full(none.shape, FAR, BF16)
        values_ref[pair, cache_count:tree_end, :QDIM] = tree_pairs[:, kcol + QDIM : kcol + 2 * QDIM]
        values_ref[pair, tree_end:, :QDIM] = none
    for load in loads[5:]:
        load.wait()
    for pair in range(pair_heads):
        first = pair * group_size * QDIM
        query = ordered(query_start + first, group_size * QDIM).astype(BF16)
        query = jnp.concatenate(
            [
                jnp.concatenate([query[:, g * QDIM : (g + 1) * QDIM], own_node], axis=1)
                for g in range(group_size)
            ],
            axis=0,
        )
        score_ref[...] = last_dot(query, keys_ref[pair])
        for start in range(0, group_size * nodes, 16):
            rows = slice(start, start + 16)
            score = score_ref[rows, :]
            peak = jnp.max(score, axis=1, keepdims=True)
            prob_ref[rows, :] = jnp.exp2((score - peak) * scale).astype(BF16)
        for g in range(0, group_size, 2):
            rows = slice(g * nodes, (g + 2) * nodes)
            result = jnp.dot(prob_ref[rows, :], values_ref[pair], preferred_element_type=F32)
            result = (result[:, :QDIM] / result[:, QDIM:]).astype(BF16)
            for part in range(2):
                column = first + (g + part) * QDIM
                attend_ref[:, column : column + QDIM] = result[part * nodes : (part + 1) * nodes]


def mix(first_offsets, second_offsets, late, *refs):
    firsts, refs = tuple(zip(refs, first_offsets)), refs[len(first_offsets) :]
    seconds, refs = tuple(zip(refs, second_offsets)), refs[len(second_offsets) :]
    order_ref, weight_ref, base_ref, skip_ref, attend_ref = refs[:5]
    mixed_ref, square_ref, input_ref, attend_hbm, sem = refs[5:]
    store = pltpu.make_async_copy(attend_ref, attend_hbm, sem)
    store.start()
    nodes, width = base_ref.shape
    order = order_ref[...]
    sub = lax.broadcasted_iota(jnp.int32, (2 * nodes, LANES), 0) < nodes
    lane = lax.broadcasted_iota(jnp.int32, (2 * nodes, LANES), 1) < HEAD_DIM
    same = sub == lane
    total = jnp.zeros((nodes, LANES), F32)
    chunk = 4 * LANES

    def ordered(start):
        views = seconds if start < late else firsts
        return jnp.dot(order, joined(views, start, chunk), preferred_element_type=F32)

    ahead = ordered(0)
    for start in range(0, width, chunk):
        wide = ahead
        if start + chunk < width:
            ahead = ordered(start + chunk)
        rows = wide.astype(BF16)
        input_ref[:, start : start + chunk] = rows
        for begin in range(0, chunk, LANES):
            lanes = slice(start + begin, start + begin + LANES)
            one = rows[:, begin : begin + LANES]
            both = jnp.concatenate([one, one], axis=0)
            both = jnp.where(same, both, jnp.zeros_like(both))
            mixed = jnp.dot(weight_ref[:, lanes], both, preferred_element_type=F32)
            mixed = mixed + base_ref[:, lanes] + skip_ref[:, lanes] * wide[:, begin : begin + LANES]
            mixed_ref[:, lanes] = mixed
            total = total + mixed * mixed
    square_ref[...] = jnp.broadcast_to(jnp.sum(total, axis=1, keepdims=True), square_ref.shape)
    store.wait()


def advance(input_ref, path_ref, write_ref, kept_ref, out_ref):
    head_local = kept_ref.shape[0]
    groups = write_ref.shape[1] // STATE
    per_group = head_local // groups
    width = per_group * HEAD_DIM
    for group in range(groups):
        lanes = slice(group * width, (group + 1) * width)
        weighted = (path_ref[:, lanes] * input_ref[:, lanes].astype(F32)).astype(BF16)
        update = lax.dot_general(
            weighted,
            write_ref[:, group * STATE : (group + 1) * STATE],
            (((0,), (0,)), ((), ())),
            preferred_element_type=F32,
        )
        for index in range(per_group):
            head = group * per_group + index
            out_ref[0, head] = (
                kept_ref[head] + update[index * HEAD_DIM : (index + 1) * HEAD_DIM]
            ).astype(BF16)


def finish(total_width, mixed_ref, mine_ref, other_ref, gain_ref, state_ref, *refs):
    out_hbm, state_hbm, out_ref, sems = refs
    chunks = sems.shape[0] - 1
    store = pltpu.make_async_copy(state_ref, state_hbm, sems.at[chunks])
    store.start()
    square = mine_ref[...] + other_ref[...]
    scale = 1.0 / jnp.sqrt(square / total_width + 1e-05)
    width = out_ref.shape[1] // chunks
    stores = [store]
    for chunk in range(chunks):
        for start in range(chunk * width, (chunk + 1) * width, LANES):
            lanes = slice(start, start + LANES)
            out_ref[:, lanes] = (mixed_ref[:, lanes] * scale * gain_ref[:, lanes]).astype(BF16)
        view = pl.ds(chunk * width, width)
        stores.append(
            pltpu.make_async_copy(out_ref.at[:, view], out_hbm.at[:, view], sems.at[chunk])
        )
        stores[-1].start()
    for store in stores:
        store.wait()


SPACES = {"h": pltpu.HBM, "v": pltpu.VMEM, "s": pltpu.SMEM}


def call(body, ins, outs, scratch=(), mebibytes=8):
    def run(*operands):
        placed = [
            operand if space == "s" else pltpu.with_memory_space_constraint(operand, SPACES[space])
            for space, operand in zip(ins, operands, strict=True)
        ]
        return pl.pallas_call(
            body,
            out_shape=tuple(SPACES[space](dims, kind) for space, dims, kind in outs),
            in_specs=[pl.BlockSpec(memory_space=SPACES[space]) for space in ins],
            out_specs=tuple(pl.BlockSpec(memory_space=SPACES[out[0]]) for out in outs),
            scratch_shapes=scratch,
            compiler_params=pltpu.CompilerParams(vmem_limit_bytes=mebibytes * 1024 * 1024),
        )(*placed)

    return run


def local(
    draft_input,
    draft_proj,
    draft_step,
    draft_query,
    draft_keyval,
    row_target,
    tree_mask,
    accepted,
    cache_length,
    scan_state,
    cache_keyval,
    decay_rate,
    step_bias,
    skip_gain,
    norm_gain,
):
    row_count, scan_width = draft_input.shape
    peers = lax.axis_size("req")
    head_shards = lax.axis_size("head")
    cap_rows = max(2, row_count // peers)
    slot_total = peers * cap_rows
    direct = 4 <= peers <= 16 and peers & (peers - 1) == 0
    head_local = scan_width // HEAD_DIM
    query_width = draft_query.shape[1]
    keyval_width = draft_keyval.shape[1]
    proj_width = draft_proj.shape[1]
    groups = proj_width // (2 * STATE)
    all_width = scan_width + query_width + keyval_width + proj_width + LANES
    early = int(EARLY * scan_width) if direct else scan_width
    late = scan_width - early
    rest_width = all_width - late
    if direct:
        odd = range(1, peers, 2)
        even = range(2, peers, 2)
        layout = [((0, 1, 0, all_width, 0),)]
        layout += [((block, 1, late, all_width, 0),) for block in range(1, peers)]
        layout += [((block, 1, 0, late, 0),) for block in even]
        layout += [tuple((block, 1, 0, late, index * late) for index, block in enumerate(odd))]
        widths = [all_width] + [rest_width] * (peers - 1)
        widths += [late] * len(even) + [late * len(odd)]
        rows_of = cap_rows
    else:
        layout, widths = [((0, peers, 0, all_width, 0),)], [all_width]
        rows_of = slot_total
    sources = (draft_input, draft_query, draft_keyval, draft_proj, draft_step)
    packed = call(
        functools.partial(pack, (row_count, cap_rows, peers), direct, layout),
        "h" * 6,
        tuple(("v", (rows_of, width), BF16) for width in widths),
        scratch=[pltpu.VMEM((1, row_count), jnp.int32)]
        + [pltpu.VMEM(source.shape, BF16) for source in sources]
        + [pltpu.SemaphoreType.DMA((6,))],
    )(row_target.reshape(1, row_count), *sources)

    def moved(block, step):
        pairs = [(index, index ^ step) for index in range(peers)]
        return lax.ppermute(block, "req", pairs)

    if direct:
        own, rest, inputs = packed[0], packed[1:peers], packed[peers:]
        arrived = moved(inputs[-1], 1)
        rest = [moved(block, step) for step, block in enumerate(rest, start=1)]
        count = len(even)

        def forward_all(*refs):
            forward(refs[:count], refs[count], refs[count + 1 :])

        pairs = call(
            forward_all, "v" * (count + 1), (("v", (cap_rows, 2 * late), BF16),) * count
        )(*inputs[:-1], arrived)
        pairs = [moved(block, step) for step, block in zip(even, pairs)]
        first_blocks, first_offsets = [own] + rest, [0] + [late] * (peers - 1)
        second_blocks, second_offsets = [own, arrived], [0, 0]
        for block in pairs:
            second_blocks += [block, block]
            second_offsets += [0, -late]
    else:
        split = packed[0].reshape(peers, cap_rows, all_width)
        arrived = lax.all_to_all(split, "req", split_axis=0, concat_axis=0, tiled=True)
        first_blocks, first_offsets = [arrived.reshape(slot_total, all_width)], [0]
        second_blocks, second_offsets = [], []

    scalars = lax.pad(accepted, 0, [(0, LANES - 1, 0)]) + lax.pad(
        cache_length, 0, [(1, LANES - 2, 0)]
    )
    scalars = scalars.reshape(1, LANES)
    pair_heads = keyval_width // (2 * QDIM)
    score_rows = NODES * (query_width // QDIM // pair_heads)
    key_rows = cache_keyval.shape[1] + LANES
    attended, weight, base, path, kept, write, order, skip_wide, gain = call(
        functools.partial(
            middle,
            first_offsets,
            (query_width, keyval_width, proj_width, head_local, scan_width),
        ),
        "v" * (len(first_blocks) + 1) + "h" * 7,
        (
            ("v", (row_count, query_width), BF16),
            ("v", (NODES, head_local * NODES), BF16),
            ("v", (NODES, scan_width), F32),
            ("v", (NODES, scan_width), F32),
            ("v", (head_local, HEAD_DIM, STATE), F32),
            ("v", (NODES, groups * STATE), BF16),
            ("v", (NODES, slot_total), BF16),
            ("v", (1, scan_width), F32),
            ("v", (1, scan_width), F32),
        ),
        scratch=[
            pltpu.VMEM(tree_mask.shape, jnp.int32),
            pltpu.VMEM((1, head_local), F32),
            pltpu.VMEM((1, head_local), F32),
            pltpu.VMEM((1, head_local), F32),
            pltpu.VMEM(scan_state.shape, BF16),
            pltpu.VMEM((pair_heads, key_rows, 2 * QDIM), BF16),
            pltpu.VMEM((pair_heads, key_rows, 2 * QDIM), BF16),
            pltpu.VMEM((score_rows, key_rows), F32),
            pltpu.VMEM((score_rows, key_rows), BF16),
            pltpu.VMEM((2, head_local, LANES), F32),
            pltpu.SemaphoreType.DMA((6 + 2 * pair_heads,)),
        ],
        mebibytes=24,
    )(
        *first_blocks,
        scalars,
        tree_mask,
        decay_rate.reshape(1, head_local),
        step_bias.reshape(1, head_local),
        skip_gain.reshape(1, head_local),
        scan_state,
        cache_keyval,
        norm_gain.reshape(1, scan_width),
    )

    mixed, square, inputs, attend_out = call(
        functools.partial(mix, first_offsets, second_offsets, late),
        "v" * (len(first_blocks) + len(second_blocks) + 5),
        (
            ("v", (NODES, scan_width), F32),
            ("v", (NODES, LANES), F32),
            ("v", (NODES, scan_width), BF16),
            ("h", (row_count, query_width), BF16),
        ),
        scratch=[pltpu.SemaphoreType.DMA(())],
    )(*first_blocks, *second_blocks, order, weight, base, skip_wide, attended)
    swap = [(index, (index + 1) % head_shards) for index in range(head_shards)]
    other = lax.ppermute(square, "head", swap)
    new_state = call(advance, "v" * 4, (("v", scan_state.shape, BF16),))(
        inputs, path, write, kept
    )[0]
    mixer_out, new_state = call(
        functools.partial(finish, head_shards * scan_width),
        "v" * 5,
        (("h", (row_count, scan_width), BF16), ("h", scan_state.shape, BF16)),
        scratch=[pltpu.VMEM((row_count, scan_width), BF16), pltpu.SemaphoreType.DMA((5,))],
    )(mixed, square, other, gain, new_state)
    return (mixer_out, attend_out, new_state)


def solution(mesh):
    assert mesh.shape["head"] == 2
    rows = P(("grp", "req"), "head")

    return jax.shard_map(
        local,
        mesh=mesh,
        in_specs=(
            rows,
            rows,
            rows,
            rows,
            rows,
            P(("grp", "req")),
            P(("grp", "req"), None, None),
            P(("grp", "req")),
            P(("grp", "req")),
            P(("grp", "req"), "head", None, None),
            P(("grp", "req"), None, "head"),
            P("head"),
            P("head"),
            P("head"),
            P("head"),
        ),
        out_specs=(rows, rows, P(("grp", "req"), "head", None, None)),
        check_vma=False,
    )
```

```python
import functools

import jax
import jax.numpy as jnp
from jax import lax
from jax.experimental import pallas as pl
from jax.experimental.pallas import tpu as pltpu
from jax.sharding import PartitionSpec as P


HEAD_DIM = 64
STATE = 128
QDIM = 128
NODES = 64
LANES = 128
LOG2E = 1.4426950408889634
FAR = -1e30
EARLY_FROM = (8, 8, 8, 8, 0, 8, 8, 8)
SCORE_EVERY = 1
SOFT_FROM = 12
SOFT_EACH = 2
ATTEND_PARTS = 4
F32 = jnp.float32
BF16 = jnp.bfloat16


def last_dot(left, right):
    return lax.dot_general(left, right, (((1,), (1,)), ((), ())), preferred_element_type=F32)


def row_to_column(row):
    size = row.shape[1]
    sub = lax.broadcasted_iota(jnp.int32, (size, size), 0)
    lane = lax.broadcasted_iota(jnp.int32, (size, size), 1)
    spread = jnp.broadcast_to(row, (size, size))
    return jnp.sum(jnp.where(sub == lane, spread, jnp.zeros_like(spread)), axis=1, keepdims=True)


def slot_one_hot(target, row_count, cap_rows, slot_total, me):
    shift = row_count.bit_length() - 1
    peer = lax.shift_right_logical(target, jnp.full_like(target, shift))
    local = target - peer * row_count
    peer_f = peer.astype(F32)
    peer_col = row_to_column(peer_f)
    size = row_count
    sub = lax.broadcasted_iota(jnp.int32, (size, size), 0)
    lane = lax.broadcasted_iota(jnp.int32, (size, size), 1)
    same = jnp.logical_and(peer_col == peer_f, sub < lane)
    rank = jnp.sum(jnp.where(same, 1.0, 0.0), axis=0, keepdims=True).astype(jnp.int32)
    block = peer if me is None else jnp.bitwise_xor(peer, jnp.full_like(peer, me))
    slot = block * cap_rows + rank
    slots = lax.broadcasted_iota(jnp.int32, (slot_total, size), 0)
    return jnp.where(slots == slot, 1.0, 0.0).astype(BF16), local


def pack(sizes, xor_blocks, layout, *refs):
    row_count, cap_rows, block_count = sizes
    target_hbm, sources, refs = refs[0], refs[1:6], refs[6:]
    outs, held_target, held, sems = refs[:-7], refs[-7], refs[-6:-1], refs[-1]
    target_copy = pltpu.make_async_copy(target_hbm, held_target, sems.at[5])
    target_copy.start()
    copies = [
        pltpu.make_async_copy(source, buffer, sems.at[index])
        for index, (source, buffer) in enumerate(zip(sources, held))
    ]
    for copy in copies[1:] + copies[:1]:
        copy.start()
    me = lax.axis_index("req") if xor_blocks else None
    slot_total = block_count * cap_rows
    target_copy.wait()
    chosen, local = slot_one_hot(held_target[...], row_count, cap_rows, slot_total, me)
    columns = [0]
    for buffer in held:
        columns.append(columns[-1] + buffer.shape[1])
    for index in list(range(1, len(held))) + [0]:
        copies[index].wait()
        part = held[index][...]
        column = columns[index]
        if index == len(held) - 1:
            local_col = row_to_column((local + 1).astype(F32))
            labels = jnp.broadcast_to(local_col, (row_count, LANES - part.shape[1])).astype(BF16)
            part = jnp.concatenate([part, labels], axis=1)
        for begin in range(0, part.shape[1], 4 * LANES):
            piece = part[:, begin : begin + 4 * LANES]
            width = piece.shape[1]
            moved = jnp.dot(chosen, piece, preferred_element_type=F32).astype(BF16)
            for out_ref, pieces in zip(outs, layout):
                for first_block, blocks, start, end, at in pieces:
                    if start <= column < end:
                        rows = slice(first_block * cap_rows, (first_block + blocks) * cap_rows)
                        place = column - start + at
                        out_ref[:, place : place + width] = moved[rows]
            column += width


def forward(widths, arrived_ref, starts, own_refs, out_refs):
    for (own, more), start, own_ref, out_ref in zip(widths, starts, own_refs, out_refs):
        if own:
            out_ref[:, :own] = own_ref[:, :own]
        if more:
            out_ref[:, own:] = arrived_ref[:, start : start + more]


def joined(views, start, width):
    parts = [ref[:, start - offset : start - offset + width] for ref, offset in views]
    return parts[0] if len(parts) == 1 else jnp.concatenate(parts, axis=0)


def spread(table, column):
    half = lax.broadcasted_iota(jnp.int32, table.shape, 1) // HEAD_DIM
    return jnp.take_along_axis(table, half + column, axis=1, mode="promise_in_bounds")


def middle(offsets, sizes, *refs):
    query_width, keyval_width, proj_width, head_local, query_start = sizes
    blocks, refs = tuple(zip(refs, offsets)), refs[len(offsets) :]
    scalar_ref, mask_hbm, decay_hbm, bias_hbm, skip_hbm, state_hbm, cache_hbm, gain_hbm = refs[:8]
    attend_ref, weight_ref, base_ref, columns_ref, keep_ref = refs[8:13]
    write_ref, order_ref, skip_out_ref, gain_ref = refs[13:17]
    state_ref, mask_ref, decay_ref, bias_ref, skip_ref, keys_ref, values_ref = refs[17:24]
    query_ref, score_ref, prob_ref, rows_ref, sems = refs[24:]
    pair_heads = keyval_width // (2 * QDIM)
    cache_count = cache_hbm.shape[1]
    sources = [mask_hbm, decay_hbm, bias_hbm, skip_hbm]
    targets = [mask_ref, decay_ref, bias_ref, skip_ref]
    for pair in range(pair_heads):
        for part, held in enumerate((keys_ref, values_ref)):
            sources.append(cache_hbm.at[0, :, pl.ds((2 * pair + part) * QDIM, QDIM)])
            targets.append(held.at[pair, pl.ds(0, cache_count), pl.ds(0, QDIM)])
    sources += [state_hbm, gain_hbm]
    targets += [state_ref, gain_ref]
    loads = [
        pltpu.make_async_copy(source, held, sems.at[index])
        for index, (source, held) in enumerate(zip(sources, targets))
    ]
    for load in loads:
        load.start()
    nodes = mask_ref.shape[1]
    kv_start = query_start + query_width
    proj_start = kv_start + keyval_width
    step_start = proj_start + proj_width
    tail = joined(blocks, step_start, LANES)
    label_lane = tail[:, LANES - nodes :].astype(F32)
    slot_total = tail.shape[0]
    node_lane = lax.broadcasted_iota(jnp.int32, (slot_total, nodes), 1).astype(F32) + 1.0
    order = jnp.where(label_lane == node_lane, 1.0, 0.0).T.astype(BF16)
    order_ref[...] = order

    def ordered(start, width):
        return jnp.dot(order, joined(blocks, start, width), preferred_element_type=F32)

    length = scalar_ref[0:1, 1:2]
    position = lax.broadcasted_iota(jnp.int32, (1, cache_count), 1)
    cache_bias = jnp.where(position < length, 0.0, FAR)
    for pair in range(pair_heads):
        values_ref[pair, :, QDIM:] = jnp.ones((values_ref.shape[1], LANES), BF16)

    for load in loads[:4]:
        load.wait()
    mask_float = mask_ref[0].astype(F32)
    raw = ordered(step_start, LANES)[:, :head_local] + bias_ref[...]
    step = jnp.maximum(raw, 0.0) + jnp.log1p(jnp.exp(-jnp.abs(raw)))
    cumulative = jnp.dot(
        mask_float,
        (-LOG2E * decay_ref[...]) * step,
        precision=lax.Precision.HIGHEST,
        preferred_element_type=F32,
    )
    cumulative_t = cumulative.T
    step_t = step.T
    accepted = scalar_ref[0:1, 0:1]
    node_sub = lax.broadcasted_iota(jnp.int32, (nodes, head_local), 0)
    lane_of = lax.broadcasted_iota(jnp.int32, (head_local, nodes), 1)
    pick = jnp.sum(jnp.where(node_sub == accepted, cumulative, 0.0), axis=0, keepdims=True)
    node_lanes = lax.broadcasted_iota(jnp.int32, (nodes, nodes), 1)
    mask_t = mask_float.T
    mask_pick = jnp.sum(jnp.where(node_lanes == accepted, mask_t, 0.0), axis=1, keepdims=True)
    path = mask_pick * jnp.exp2(jnp.minimum(pick - cumulative, 0.0)) * step
    pick_col = jnp.sum(jnp.where(lane_of == accepted, cumulative_t, 0.0), axis=1, keepdims=True)
    keep_ref[...] = jnp.broadcast_to(jnp.exp2(pick_col), (head_local, LANES))

    groups = proj_width // (2 * STATE)
    per_group = head_local // groups
    wide = LANES // HEAD_DIM
    pairs = head_local // wide
    low = lax.broadcasted_iota(jnp.int32, (pairs, LANES), 1) < HEAD_DIM
    rows_ref[0] = jnp.concatenate([cumulative_t] * wide, axis=1)
    rows_ref[1] = jnp.concatenate([step_t] * wide, axis=1)

    def pair_rows(index):
        even = rows_ref[index, pl.ds(0, pairs, stride=2), :]
        odd = rows_ref[index, pl.ds(1, pairs, stride=2), :]
        return jnp.where(low, even, odd)

    decay_pairs, step_pairs = pair_rows(0), pair_rows(1)
    columns = jnp.concatenate([cumulative, path], axis=1)
    columns_ref[...] = columns
    skip_columns = jnp.broadcast_to(
        jnp.concatenate([skip_ref[...]] * wide, axis=1), (8, LANES)
    )
    group_size = query_width // QDIM // pair_heads
    scale = QDIM ** (-0.5) * LOG2E
    tree_pairs = ordered(kv_start, keyval_width).astype(BF16)
    none = jnp.zeros((keys_ref.shape[1] - cache_count - nodes, QDIM), BF16)
    tree_bias = (1.0 - mask_float) * FAR
    past = jnp.full((nodes, keys_ref.shape[1] - cache_count - nodes), FAR, F32)
    tree_bias = jnp.concatenate([tree_bias, past], axis=1)
    tree_end = cache_count + nodes
    for pair in range(pair_heads):
        kcol = pair * 2 * QDIM
        keys_ref[pair, cache_count:tree_end, :] = tree_pairs[:, kcol : kcol + QDIM]
        keys_ref[pair, tree_end:, :] = none
        values_ref[pair, cache_count:tree_end, :QDIM] = tree_pairs[:, kcol + QDIM : kcol + 2 * QDIM]
        values_ref[pair, tree_end:, :QDIM] = none
        first = query_start + pair * group_size * QDIM
        query = ordered(first, group_size * QDIM).astype(BF16)
        for g in range(group_size):
            rows = slice(g * nodes, (g + 1) * nodes)
            query_ref[pair, rows, :] = query[:, g * QDIM : (g + 1) * QDIM]

    row_total = group_size * nodes

    def score(pair, block):
        keys = slice(block * LANES, (block + 1) * LANES)
        score_ref[pair, :, keys] = last_dot(query_ref[pair], keys_ref[pair, keys, :])

    def soften(pair, start):
        rows = slice(start, start + 16)
        node = start % nodes
        cached = score_ref[pair, rows, :cache_count] + cache_bias
        tree = score_ref[pair, rows, cache_count:] + tree_bias[node : node + 16]
        part = jnp.concatenate([cached, tree], axis=1)
        peak = jnp.max(part, axis=1, keepdims=True)
        prob_ref[pair, rows, :] = jnp.exp2((part - peak) * scale).astype(BF16)

    def attend(pair, start, count):
        rows = slice(start, start + count)
        result = jnp.dot(prob_ref[pair, rows, :], values_ref[pair], preferred_element_type=F32)
        result = (result[:, :QDIM] / result[:, QDIM:]).astype(BF16)
        for begin in range(0, count, nodes):
            column = (pair * group_size + (start + begin) // nodes) * QDIM
            attend_ref[:, column : column + QDIM] = result[begin : begin + nodes]

    for load in loads[4:]:
        load.wait()
    key_blocks = keys_ref.shape[1] // LANES
    scores = [(pair, block) for pair in range(pair_heads) for block in range(key_blocks)]
    softs = [(pair, start) for pair in range(pair_heads) for start in range(0, row_total, 16)]
    per_pair = row_total // 16
    done_softs = 0
    for group in range(groups):
        proj = ordered(proj_start + group * 2 * STATE, 2 * STATE).astype(BF16)
        write_rows = proj[:, :STATE]
        read_rows = proj[:, STATE:]
        write_ref[:, group * STATE : (group + 1) * STATE] = write_rows
        inner = last_dot(read_rows, write_rows) * mask_float
        inner = jnp.concatenate([inner] * wide, axis=1)
        for pair in range(per_group // wide):
            head = group * per_group + pair * wide
            lanes = slice(head * HEAD_DIM, head * HEAD_DIM + LANES)
            row = slice(head // wide, head // wide + 1)
            state = state_ref[0, head : head + wide].reshape(wide * HEAD_DIM, STATE)
            carried = last_dot(read_rows, state)
            decay_i = spread(columns, head)
            weight = jnp.exp2(jnp.minimum(decay_i - decay_pairs[row], 0.0))
            weight_ref[:, lanes] = (weight * inner * step_pairs[row]).astype(BF16)
            base_ref[:, lanes] = jnp.exp2(decay_i) * carried
            skip_out_ref[:, lanes] = spread(skip_columns, head)[0:1]
            step_index = head // wide
            if SCORE_EVERY and step_index % SCORE_EVERY == 0 and scores:
                score(*scores.pop(0))
            if SOFT_FROM <= step_index:
                for _ in range(SOFT_EACH):
                    if done_softs < per_pair:
                        soften(*softs[done_softs])
                        done_softs += 1
    while scores:
        score(*scores.pop(0))
    while done_softs < per_pair:
        soften(*softs[done_softs])
        done_softs += 1
    half_rows = row_total // ATTEND_PARTS
    for pair in range(pair_heads):
        ahead = softs[done_softs : done_softs + per_pair]
        done_softs += per_pair
        share = -(-len(ahead) // ATTEND_PARTS)
        for part in range(ATTEND_PARTS):
            attend(pair, part * half_rows, half_rows)
            for item in ahead[part * share : (part + 1) * share]:
                soften(*item)


def mix(first_offsets, second_offsets, late, *refs):
    firsts, refs = tuple(zip(refs, first_offsets)), refs[len(first_offsets) :]
    seconds, refs = tuple(zip(refs, second_offsets)), refs[len(second_offsets) :]
    order_ref, weight_ref, base_ref, skip_ref, attend_ref = refs[:5]
    mixed_ref, square_ref, input_ref, attend_hbm, sem = refs[5:]
    store = pltpu.make_async_copy(attend_ref, attend_hbm, sem)
    store.start()
    nodes, width = base_ref.shape
    order = order_ref[...]
    sub = lax.broadcasted_iota(jnp.int32, (2 * nodes, LANES), 0) < nodes
    lane = lax.broadcasted_iota(jnp.int32, (2 * nodes, LANES), 1) < HEAD_DIM
    same = sub == lane
    total = jnp.zeros((nodes, LANES), F32)
    chunk = 4 * LANES

    def ordered(start):
        views = firsts
        if seconds:
            views = [
                second if start < early_from else first
                for first, second, early_from in zip(firsts, seconds, late)
            ]
        return jnp.dot(order, joined(views, start, chunk), preferred_element_type=F32)

    ahead = ordered(0)
    for start in range(0, width, chunk):
        wide = ahead
        if start + chunk < width:
            ahead = ordered(start + chunk)
        rows = wide.astype(BF16)
        input_ref[:, start : start + chunk] = rows
        for begin in range(0, chunk, LANES):
            lanes = slice(start + begin, start + begin + LANES)
            one = rows[:, begin : begin + LANES]
            both = jnp.concatenate([one, one], axis=0)
            both = jnp.where(same, both, jnp.zeros_like(both))
            mixed = jnp.dot(weight_ref[:, lanes], both, preferred_element_type=F32)
            mixed = mixed + base_ref[:, lanes] + skip_ref[:, lanes] * wide[:, begin : begin + LANES]
            mixed_ref[:, lanes] = mixed
            total = total + mixed * mixed
    square_ref[...] = jnp.broadcast_to(jnp.sum(total, axis=1, keepdims=True), square_ref.shape)
    store.wait()


def advance(input_ref, columns_ref, write_ref, keep_ref, state_ref, out_ref):
    head_local = state_ref.shape[1]
    groups = write_ref.shape[1] // STATE
    per_group = head_local // groups
    wide = LANES // HEAD_DIM
    columns = columns_ref[...]
    for group in range(groups):
        weighted = []
        for pair in range(per_group // wide):
            head = group * per_group + pair * wide
            rows = input_ref[:, head * HEAD_DIM : head * HEAD_DIM + LANES].astype(F32)
            weighted.append((spread(columns, head_local + head) * rows).astype(BF16))
        update = lax.dot_general(
            jnp.concatenate(weighted, axis=1),
            write_ref[:, group * STATE : (group + 1) * STATE],
            (((0,), (0,)), ((), ())),
            preferred_element_type=F32,
        )
        for index in range(per_group):
            head = group * per_group + index
            kept = keep_ref[head : head + 1, :] * state_ref[0, head].astype(F32)
            out_ref[0, head] = (kept + update[index * HEAD_DIM : (index + 1) * HEAD_DIM]).astype(BF16)


def finish(total_width, mixed_ref, mine_ref, other_ref, gain_ref, state_ref, *refs):
    out_hbm, state_hbm, out_ref, sems = refs
    chunks = sems.shape[0] - 1
    store = pltpu.make_async_copy(state_ref, state_hbm, sems.at[chunks])
    store.start()
    square = mine_ref[...] + other_ref[...]
    scale = 1.0 / jnp.sqrt(square / total_width + 1e-05)
    width = out_ref.shape[1] // chunks
    stores = [store]
    for chunk in range(chunks):
        for start in range(chunk * width, (chunk + 1) * width, LANES):
            lanes = slice(start, start + LANES)
            out_ref[:, lanes] = (mixed_ref[:, lanes] * scale * gain_ref[:, lanes]).astype(BF16)
        view = pl.ds(chunk * width, width)
        stores.append(
            pltpu.make_async_copy(out_ref.at[:, view], out_hbm.at[:, view], sems.at[chunk])
        )
        stores[-1].start()
    for store in stores:
        store.wait()


SPACES = {"h": pltpu.HBM, "v": pltpu.VMEM, "s": pltpu.SMEM}


def call(body, ins, outs, scratch=(), mebibytes=8):
    def run(*operands):
        placed = [
            operand if space == "s" else pltpu.with_memory_space_constraint(operand, SPACES[space])
            for space, operand in zip(ins, operands, strict=True)
        ]
        return pl.pallas_call(
            body,
            out_shape=tuple(SPACES[space](dims, kind) for space, dims, kind in outs),
            in_specs=[pl.BlockSpec(memory_space=SPACES[space]) for space in ins],
            out_specs=tuple(pl.BlockSpec(memory_space=SPACES[out[0]]) for out in outs),
            scratch_shapes=scratch,
            compiler_params=pltpu.CompilerParams(vmem_limit_bytes=mebibytes * 1024 * 1024),
        )(*placed)

    return run


def local(
    draft_input,
    draft_proj,
    draft_step,
    draft_query,
    draft_keyval,
    row_target,
    tree_mask,
    accepted,
    cache_length,
    scan_state,
    cache_keyval,
    decay_rate,
    step_bias,
    skip_gain,
    norm_gain,
):
    row_count, scan_width = draft_input.shape
    peers = lax.axis_size("req")
    head_shards = lax.axis_size("head")
    cap_rows = max(2, row_count // peers)
    slot_total = peers * cap_rows
    direct = peers == len(EARLY_FROM)
    assert row_count & (row_count - 1) == 0 and scan_width * 2 == LANES * HEAD_DIM
    head_local = scan_width // HEAD_DIM
    query_width = draft_query.shape[1]
    keyval_width = draft_keyval.shape[1]
    proj_width = draft_proj.shape[1]
    groups = proj_width // (2 * STATE)
    all_width = scan_width + query_width + keyval_width + proj_width + LANES
    late = 0
    if direct:
        odd = range(1, peers, 2)
        even = range(2, peers, 2)
        unit = scan_width // 8
        early_from = [EARLY_FROM[block] * unit for block in range(peers)]
        layout = [((0, 1, 0, all_width, 0),)]
        layout += [((block, 1, early_from[block], all_width, 0),) for block in range(2, peers)]
        layout += [((block, 1, 0, early_from[block], 0),) for block in even]
        side, side_width = [(1, 1, 0, all_width, 0)], all_width
        for block in odd[1:]:
            side.append((block, 1, 0, early_from[block], side_width))
            side_width += early_from[block]
        layout += [tuple(side)]
        widths = [all_width] + [all_width - early_from[block] for block in range(2, peers)]
        widths += [max(early_from[block], LANES) for block in even] + [side_width]
        rows_of = cap_rows
    else:
        layout, widths = [((0, peers, 0, all_width, 0),)], [all_width]
        rows_of = slot_total
    sources = (draft_input, draft_query, draft_keyval, draft_proj, draft_step)
    packed = call(
        functools.partial(pack, (row_count, cap_rows, peers), direct, layout),
        "h" * 6,
        tuple(("v", (rows_of, width), BF16) for width in widths),
        scratch=[pltpu.VMEM((1, row_count), jnp.int32)]
        + [pltpu.VMEM(source.shape, BF16) for source in sources]
        + [pltpu.SemaphoreType.DMA((6,))],
    )(row_target.reshape(1, row_count), *sources)

    def moved(block, step):
        pairs = [(index, index ^ step) for index in range(peers)]
        return lax.ppermute(block, "req", pairs)

    if direct:
        own, rest, inputs = packed[0], packed[1 : peers - 1], packed[peers - 1 :]
        arrived = moved(inputs[-1], 1)
        rest = [moved(block, step) for step, block in enumerate(rest, start=2)]
        later = [block for block in even if early_from[block] + early_from[block + 1]]
        inputs = {block: part for block, part in zip(even, inputs)}
        count = len(later)

        def forward_all(accepted_ref, length_ref, *refs):
            widths = [(early_from[block], early_from[block + 1]) for block in later]
            skips = [sum(early_from[3:block:2]) for block in later]
            forward(widths, refs[count], [all_width + skip for skip in skips], refs[:count], refs[count + 1 : -1])
            lane = lax.broadcasted_iota(jnp.int32, refs[-1].shape, 1)
            refs[-1][...] = jnp.where(lane == 0, accepted_ref[0], length_ref[0])

        *pairs, scalars = call(
            forward_all,
            "ss" + "v" * (count + 1),
            tuple(
                ("v", (cap_rows, early_from[block] + early_from[block + 1]), BF16)
                for block in later
            )
            + (("v", (8, LANES), jnp.int32),),
        )(accepted, cache_length, *[inputs[block] for block in later], arrived)
        pairs = {block: moved(part, block) for block, part in zip(later, pairs)}
        first_blocks, first_offsets = [own, arrived] + rest, [0, 0] + early_from[2:]
        second_blocks, second_offsets = [own, arrived], [0, 0]
        for step in even:
            block = pairs.get(step, own)
            second_blocks += [block, block]
            second_offsets += [0, -early_from[step]]
        late = early_from
    else:
        split = packed[0].reshape(peers, cap_rows, all_width)
        arrived = lax.all_to_all(split, "req", split_axis=0, concat_axis=0, tiled=True)
        first_blocks, first_offsets = [arrived.reshape(slot_total, all_width)], [0]
        scalars = lax.pad(accepted, 0, [(0, LANES - 1, 0)])
        scalars = scalars + lax.pad(cache_length, 0, [(1, LANES - 2, 0)])
        scalars = jnp.broadcast_to(scalars, (8, LANES))
        second_blocks, second_offsets = [], []

    pair_heads = keyval_width // (2 * QDIM)
    score_rows = NODES * (query_width // QDIM // pair_heads)
    key_rows = cache_keyval.shape[1] + LANES
    attended, weight, base, columns, keep, write, order, skip_wide, gain, state = call(
        functools.partial(
            middle,
            first_offsets,
            (query_width, keyval_width, proj_width, head_local, scan_width),
        ),
        "v" * (len(first_blocks) + 1) + "h" * 7,
        (
            ("v", (row_count, query_width), BF16),
            ("v", (NODES, head_local * NODES), BF16),
            ("v", (NODES, scan_width), F32),
            ("v", (NODES, LANES), F32),
            ("v", (head_local, LANES), F32),
            ("v", (NODES, groups * STATE), BF16),
            ("v", (NODES, slot_total), BF16),
            ("v", (1, scan_width), F32),
            ("v", (1, scan_width), F32),
            ("v", scan_state.shape, BF16),
        ),
        scratch=[
            pltpu.VMEM(tree_mask.shape, jnp.int32),
            pltpu.VMEM((1, head_local), F32),
            pltpu.VMEM((1, head_local), F32),
            pltpu.VMEM((1, head_local), F32),
            pltpu.VMEM((pair_heads, key_rows, QDIM), BF16),
            pltpu.VMEM((pair_heads, key_rows, 2 * QDIM), BF16),
            pltpu.VMEM((pair_heads, score_rows, QDIM), BF16),
            pltpu.VMEM((pair_heads, score_rows, key_rows), F32),
            pltpu.VMEM((pair_heads, score_rows, key_rows), BF16),
            pltpu.VMEM((2, head_local, LANES), F32),
            pltpu.SemaphoreType.DMA((6 + 2 * pair_heads,)),
        ],
        mebibytes=28,
    )(
        *first_blocks,
        scalars,
        tree_mask,
        decay_rate.reshape(1, head_local),
        step_bias.reshape(1, head_local),
        skip_gain.reshape(1, head_local),
        scan_state,
        cache_keyval,
        norm_gain.reshape(1, scan_width),
    )

    mixed, square, inputs, attend_out = call(
        functools.partial(mix, first_offsets, second_offsets, late),
        "v" * (len(first_blocks) + len(second_blocks) + 5),
        (
            ("v", (NODES, scan_width), F32),
            ("v", (NODES, LANES), F32),
            ("v", (NODES, scan_width), BF16),
            ("h", (row_count, query_width), BF16),
        ),
        scratch=[pltpu.SemaphoreType.DMA(())],
    )(*first_blocks, *second_blocks, order, weight, base, skip_wide, attended)
    swap = [(index, (index + 1) % head_shards) for index in range(head_shards)]
    other = lax.ppermute(square, "head", swap)
    new_state = call(advance, "v" * 5, (("v", scan_state.shape, BF16),))(
        inputs, columns, write, keep, state
    )[0]
    mixer_out, new_state = call(
        functools.partial(finish, head_shards * scan_width),
        "v" * 5,
        (("h", (row_count, scan_width), BF16), ("h", scan_state.shape, BF16)),
        scratch=[pltpu.VMEM((row_count, scan_width), BF16), pltpu.SemaphoreType.DMA((5,))],
    )(mixed, square, other, gain, new_state)
    return (mixer_out, attend_out, new_state)


def solution(mesh):
    assert mesh.shape["head"] == 2
    rows = P(("grp", "req"), "head")

    return jax.shard_map(
        local,
        mesh=mesh,
        in_specs=(
            rows,
            rows,
            rows,
            rows,
            rows,
            P(("grp", "req")),
            P(("grp", "req"), None, None),
            P(("grp", "req")),
            P(("grp", "req")),
            P(("grp", "req"), "head", None, None),
            P(("grp", "req"), None, "head"),
            P("head"),
            P("head"),
            P("head"),
            P("head"),
        ),
        out_specs=(rows, rows, P(("grp", "req"), "head", None, None)),
        check_vma=False,
    )
```

```python
import functools

import jax
import jax.numpy as jnp
from jax import lax
from jax.experimental import pallas as pl
from jax.experimental.pallas import tpu as pltpu
from jax.sharding import PartitionSpec as P


HEAD_DIM = 64
STATE = 128
QDIM = 128
NODES = 64
LANES = 128
LOG2E = 1.4426950408889634
FAR = -1e30
EARLY_FROM = (8, 8, 8, 7, 0, 8, 8, 8)
SCORE_EVERY = 1
SOFT_FROM = 12
SOFT_EACH = 2
ATTEND_PARTS = 2
F32 = jnp.float32
BF16 = jnp.bfloat16


def last_dot(left, right):
    return lax.dot_general(left, right, (((1,), (1,)), ((), ())), preferred_element_type=F32)


def row_to_column(row):
    size = row.shape[1]
    sub = lax.broadcasted_iota(jnp.int32, (size, size), 0)
    lane = lax.broadcasted_iota(jnp.int32, (size, size), 1)
    spread = jnp.broadcast_to(row, (size, size))
    return jnp.sum(jnp.where(sub == lane, spread, jnp.zeros_like(spread)), axis=1, keepdims=True)


def slot_one_hot(target, row_count, cap_rows, slot_total, me):
    shift = row_count.bit_length() - 1
    peer = lax.shift_right_logical(target, jnp.full_like(target, shift))
    local = target - peer * row_count
    peer_f = peer.astype(F32)
    peer_col = row_to_column(peer_f)
    size = row_count
    sub = lax.broadcasted_iota(jnp.int32, (size, size), 0)
    lane = lax.broadcasted_iota(jnp.int32, (size, size), 1)
    same = jnp.logical_and(peer_col == peer_f, sub < lane)
    rank = jnp.sum(jnp.where(same, 1.0, 0.0), axis=0, keepdims=True).astype(jnp.int32)
    block = peer if me is None else jnp.bitwise_xor(peer, jnp.full_like(peer, me))
    slot = block * cap_rows + rank
    slots = lax.broadcasted_iota(jnp.int32, (slot_total, size), 0)
    return jnp.where(slots == slot, 1.0, 0.0).astype(BF16), local


def pack(sizes, xor_blocks, layout, *refs):
    row_count, cap_rows, block_count = sizes
    target_hbm, sources, refs = refs[0], refs[1:6], refs[6:]
    outs, held_target, held, sems = refs[:-7], refs[-7], refs[-6:-1], refs[-1]
    target_copy = pltpu.make_async_copy(target_hbm, held_target, sems.at[5])
    target_copy.start()
    copies = [
        pltpu.make_async_copy(source, buffer, sems.at[index])
        for index, (source, buffer) in enumerate(zip(sources, held))
    ]
    for copy in copies[1:] + copies[:1]:
        copy.start()
    me = lax.axis_index("req") if xor_blocks else None
    slot_total = block_count * cap_rows
    target_copy.wait()
    chosen, local = slot_one_hot(held_target[...], row_count, cap_rows, slot_total, me)
    columns = [0]
    for buffer in held:
        columns.append(columns[-1] + buffer.shape[1])
    for index in list(range(1, len(held))) + [0]:
        copies[index].wait()
        part = held[index][...]
        column = columns[index]
        if index == len(held) - 1:
            local_col = row_to_column((local + 1).astype(F32))
            labels = jnp.broadcast_to(local_col, (row_count, LANES - part.shape[1])).astype(BF16)
            part = jnp.concatenate([part, labels], axis=1)
        for begin in range(0, part.shape[1], 4 * LANES):
            piece = part[:, begin : begin + 4 * LANES]
            width = piece.shape[1]
            moved = jnp.dot(chosen, piece, preferred_element_type=F32).astype(BF16)
            for out_ref, pieces in zip(outs, layout):
                for first_block, blocks, start, end, at in pieces:
                    if start <= column < end:
                        rows = slice(first_block * cap_rows, (first_block + blocks) * cap_rows)
                        place = column - start + at
                        out_ref[:, place : place + width] = moved[rows]
            column += width


def forward(widths, arrived_ref, starts, own_refs, out_refs):
    for (own, more), start, own_ref, out_ref in zip(widths, starts, own_refs, out_refs):
        if own:
            out_ref[:, :own] = own_ref[:, :own]
        if more:
            out_ref[:, own:] = arrived_ref[:, start : start + more]


def joined(views, start, width):
    parts = [ref[:, start - offset : start - offset + width] for ref, offset in views]
    return parts[0] if len(parts) == 1 else jnp.concatenate(parts, axis=0)


def spread(table, column):
    half = lax.broadcasted_iota(jnp.int32, table.shape, 1) // HEAD_DIM
    return jnp.take_along_axis(table, half + column, axis=1, mode="promise_in_bounds")


def middle(offsets, sizes, *refs):
    query_width, keyval_width, proj_width, head_local, query_start = sizes
    blocks, refs = tuple(zip(refs, offsets)), refs[len(offsets) :]
    scalar_ref, mask_hbm, decay_hbm, bias_hbm, skip_hbm, state_hbm, cache_hbm, gain_hbm = refs[:8]
    attend_ref, weight_ref, base_ref, columns_ref, keep_ref = refs[8:13]
    write_ref, order_ref, skip_out_ref, gain_ref = refs[13:17]
    state_ref, mask_ref, decay_ref, bias_ref, skip_ref, keys_ref, values_ref = refs[17:24]
    query_ref, score_ref, prob_ref, total_ref, rows_ref, sems = refs[24:]
    pair_heads = keyval_width // (2 * QDIM)
    cache_count = cache_hbm.shape[1]
    sources = [mask_hbm, decay_hbm, bias_hbm, skip_hbm]
    targets = [mask_ref, decay_ref, bias_ref, skip_ref]
    for pair in range(pair_heads):
        for part, held in enumerate((keys_ref, values_ref)):
            sources.append(cache_hbm.at[0, :, pl.ds((2 * pair + part) * QDIM, QDIM)])
            targets.append(held.at[pair, pl.ds(0, cache_count), pl.ds(0, QDIM)])
    sources += [state_hbm, gain_hbm]
    targets += [state_ref, gain_ref]
    loads = [
        pltpu.make_async_copy(source, held, sems.at[index])
        for index, (source, held) in enumerate(zip(sources, targets))
    ]
    for load in loads:
        load.start()
    nodes = mask_ref.shape[1]
    kv_start = query_start + query_width
    proj_start = kv_start + keyval_width
    step_start = proj_start + proj_width
    tail = joined(blocks, step_start, LANES)
    label_lane = tail[:, LANES - nodes :].astype(F32)
    slot_total = tail.shape[0]
    node_lane = lax.broadcasted_iota(jnp.int32, (slot_total, nodes), 1).astype(F32) + 1.0
    order = jnp.where(label_lane == node_lane, 1.0, 0.0).T.astype(BF16)
    order_ref[...] = order

    def ordered(start, width):
        return jnp.dot(order, joined(blocks, start, width), preferred_element_type=F32)

    length = scalar_ref[0:1, 1:2]
    position = lax.broadcasted_iota(jnp.int32, (1, cache_count), 1)
    cache_bias = jnp.where(position < length, 0.0, FAR)

    for load in loads[:4]:
        load.wait()
    mask_float = mask_ref[0].astype(F32)
    raw = ordered(step_start, LANES)[:, :head_local] + bias_ref[...]
    step = jnp.maximum(raw, 0.0) + jnp.log1p(jnp.exp(-jnp.abs(raw)))
    cumulative = jnp.dot(
        mask_float,
        (-LOG2E * decay_ref[...]) * step,
        precision=lax.Precision.HIGHEST,
        preferred_element_type=F32,
    )
    cumulative_t = cumulative.T
    step_t = step.T
    accepted = scalar_ref[0:1, 0:1]
    node_sub = lax.broadcasted_iota(jnp.int32, (nodes, head_local), 0)
    lane_of = lax.broadcasted_iota(jnp.int32, (head_local, nodes), 1)
    pick = jnp.sum(jnp.where(node_sub == accepted, cumulative, 0.0), axis=0, keepdims=True)
    node_lanes = lax.broadcasted_iota(jnp.int32, (nodes, nodes), 1)
    mask_t = mask_float.T
    mask_pick = jnp.sum(jnp.where(node_lanes == accepted, mask_t, 0.0), axis=1, keepdims=True)
    path = mask_pick * jnp.exp2(jnp.minimum(pick - cumulative, 0.0)) * step
    pick_col = jnp.sum(jnp.where(lane_of == accepted, cumulative_t, 0.0), axis=1, keepdims=True)
    keep_ref[...] = jnp.broadcast_to(jnp.exp2(pick_col), (head_local, LANES))

    groups = proj_width // (2 * STATE)
    per_group = head_local // groups
    wide = LANES // HEAD_DIM
    pairs = head_local // wide
    low = lax.broadcasted_iota(jnp.int32, (pairs, LANES), 1) < HEAD_DIM
    rows_ref[0] = jnp.concatenate([cumulative_t] * wide, axis=1)
    rows_ref[1] = jnp.concatenate([step_t] * wide, axis=1)

    def pair_rows(index):
        even = rows_ref[index, pl.ds(0, pairs, stride=2), :]
        odd = rows_ref[index, pl.ds(1, pairs, stride=2), :]
        return jnp.where(low, even, odd)

    decay_pairs, step_pairs = pair_rows(0), pair_rows(1)
    columns = jnp.concatenate([cumulative, path], axis=1)
    columns_ref[...] = columns
    skip_columns = jnp.broadcast_to(
        jnp.concatenate([skip_ref[...]] * wide, axis=1), (8, LANES)
    )
    group_size = query_width // QDIM // pair_heads
    scale = QDIM ** (-0.5) * LOG2E
    tree_pairs = ordered(kv_start, keyval_width).astype(BF16)
    none = jnp.zeros((keys_ref.shape[1] - cache_count - nodes, QDIM), BF16)
    tree_bias = (1.0 - mask_float) * FAR
    past = jnp.full((nodes, keys_ref.shape[1] - cache_count - nodes), FAR, F32)
    tree_bias = jnp.concatenate([tree_bias, past], axis=1)
    tree_end = cache_count + nodes
    for pair in range(pair_heads):
        kcol = pair * 2 * QDIM
        keys_ref[pair, cache_count:tree_end, :] = tree_pairs[:, kcol : kcol + QDIM]
        keys_ref[pair, tree_end:, :] = none
        values_ref[pair, cache_count:tree_end, :] = tree_pairs[:, kcol + QDIM : kcol + 2 * QDIM]
        values_ref[pair, tree_end:, :] = none
        first = query_start + pair * group_size * QDIM
        query = ordered(first, group_size * QDIM).astype(BF16)
        for g in range(group_size):
            rows = slice(g * nodes, (g + 1) * nodes)
            query_ref[pair, rows, :] = query[:, g * QDIM : (g + 1) * QDIM]

    row_total = group_size * nodes

    def score(pair, block):
        keys = slice(block * LANES, (block + 1) * LANES)
        score_ref[pair, :, keys] = last_dot(query_ref[pair], keys_ref[pair, keys, :])

    def soften(pair, start):
        rows = slice(start, start + 16)
        node = start % nodes
        cached = score_ref[pair, rows, :cache_count] + cache_bias
        tree = score_ref[pair, rows, cache_count:] + tree_bias[node : node + 16]
        part = jnp.concatenate([cached, tree], axis=1)
        peak = jnp.max(part, axis=1, keepdims=True)
        prob = jnp.exp2((part - peak) * scale)
        total = jnp.sum(prob, axis=1, keepdims=True)
        total_ref[pair, rows, :] = jnp.broadcast_to(total, (16, QDIM))
        prob_ref[pair, rows, :] = prob.astype(BF16)

    def attend(pair, start, count):
        rows = slice(start, start + count)
        result = jnp.dot(prob_ref[pair, rows, :], values_ref[pair], preferred_element_type=F32)
        result = (result / total_ref[pair, rows, :]).astype(BF16)
        for begin in range(0, count, nodes):
            column = (pair * group_size + (start + begin) // nodes) * QDIM
            attend_ref[:, column : column + QDIM] = result[begin : begin + nodes]

    for load in loads[4:]:
        load.wait()
    key_blocks = keys_ref.shape[1] // LANES
    scores = [(pair, block) for pair in range(pair_heads) for block in range(key_blocks)]
    softs = [(pair, start) for pair in range(pair_heads) for start in range(0, row_total, 16)]
    per_pair = row_total // 16
    done_softs = 0
    for group in range(groups):
        proj = ordered(proj_start + group * 2 * STATE, 2 * STATE).astype(BF16)
        write_rows = proj[:, :STATE]
        read_rows = proj[:, STATE:]
        write_ref[:, group * STATE : (group + 1) * STATE] = write_rows
        inner = last_dot(read_rows, write_rows) * mask_float
        inner = jnp.concatenate([inner] * wide, axis=1)
        for pair in range(per_group // wide):
            head = group * per_group + pair * wide
            lanes = slice(head * HEAD_DIM, head * HEAD_DIM + LANES)
            row = slice(head // wide, head // wide + 1)
            state = state_ref[0, head : head + wide].reshape(wide * HEAD_DIM, STATE)
            carried = last_dot(read_rows, state)
            decay_i = spread(columns, head)
            weight = jnp.exp2(jnp.minimum(decay_i - decay_pairs[row], 0.0))
            weight_ref[:, lanes] = (weight * inner * step_pairs[row]).astype(BF16)
            base_ref[:, lanes] = jnp.exp2(decay_i) * carried
            skip_out_ref[:, lanes] = spread(skip_columns, head)[0:1]
            step_index = head // wide
            if SCORE_EVERY and step_index % SCORE_EVERY == 0 and scores:
                score(*scores.pop(0))
            if SOFT_FROM <= step_index:
                for _ in range(SOFT_EACH):
                    if done_softs < per_pair:
                        soften(*softs[done_softs])
                        done_softs += 1
    while scores:
        score(*scores.pop(0))
    while done_softs < per_pair:
        soften(*softs[done_softs])
        done_softs += 1
    half_rows = row_total // ATTEND_PARTS
    for pair in range(pair_heads):
        ahead = softs[done_softs : done_softs + per_pair]
        done_softs += per_pair
        share = -(-len(ahead) // ATTEND_PARTS)
        for part in range(ATTEND_PARTS):
            attend(pair, part * half_rows, half_rows)
            for item in ahead[part * share : (part + 1) * share]:
                soften(*item)


def mix(first_offsets, second_offsets, late, *refs):
    firsts, refs = tuple(zip(refs, first_offsets)), refs[len(first_offsets) :]
    seconds, refs = tuple(zip(refs, second_offsets)), refs[len(second_offsets) :]
    order_ref, weight_ref, base_ref, skip_ref, attend_ref = refs[:5]
    mixed_ref, square_ref, input_ref, attend_hbm, sem = refs[5:]
    store = pltpu.make_async_copy(attend_ref, attend_hbm, sem)
    store.start()
    nodes, width = base_ref.shape
    order = order_ref[...]
    sub = lax.broadcasted_iota(jnp.int32, (2 * nodes, LANES), 0) < nodes
    lane = lax.broadcasted_iota(jnp.int32, (2 * nodes, LANES), 1) < HEAD_DIM
    same = sub == lane
    total = jnp.zeros((nodes, LANES), F32)
    chunk = 4 * LANES

    def ordered(start):
        views = firsts
        if seconds:
            views = [
                second if start < early_from else first
                for first, second, early_from in zip(firsts, seconds, late)
            ]
        return jnp.dot(order, joined(views, start, chunk), preferred_element_type=F32)

    ahead = ordered(0)
    for start in range(0, width, chunk):
        wide = ahead
        if start + chunk < width:
            ahead = ordered(start + chunk)
        rows = wide.astype(BF16)
        input_ref[:, start : start + chunk] = rows
        for begin in range(0, chunk, LANES):
            lanes = slice(start + begin, start + begin + LANES)
            one = rows[:, begin : begin + LANES]
            both = jnp.concatenate([one, one], axis=0)
            both = jnp.where(same, both, jnp.zeros_like(both))
            mixed = jnp.dot(weight_ref[:, lanes], both, preferred_element_type=F32)
            mixed = mixed + base_ref[:, lanes] + skip_ref[:, lanes] * wide[:, begin : begin + LANES]
            mixed_ref[:, lanes] = mixed
            total = total + mixed * mixed
    square_ref[...] = jnp.broadcast_to(jnp.sum(total, axis=1, keepdims=True), square_ref.shape)
    store.wait()


def advance(input_ref, columns_ref, write_ref, keep_ref, state_ref, out_ref):
    head_local = state_ref.shape[1]
    groups = write_ref.shape[1] // STATE
    per_group = head_local // groups
    wide = LANES // HEAD_DIM
    columns = columns_ref[...]
    for group in range(groups):
        weighted = []
        for pair in range(per_group // wide):
            head = group * per_group + pair * wide
            rows = input_ref[:, head * HEAD_DIM : head * HEAD_DIM + LANES].astype(F32)
            weighted.append((spread(columns, head_local + head) * rows).astype(BF16))
        update = lax.dot_general(
            jnp.concatenate(weighted, axis=1),
            write_ref[:, group * STATE : (group + 1) * STATE],
            (((0,), (0,)), ((), ())),
            preferred_element_type=F32,
        )
        for index in range(per_group):
            head = group * per_group + index
            kept = keep_ref[head : head + 1, :] * state_ref[0, head].astype(F32)
            out_ref[0, head] = (kept + update[index * HEAD_DIM : (index + 1) * HEAD_DIM]).astype(BF16)


def finish(total_width, mixed_ref, mine_ref, other_ref, gain_ref, state_ref, *refs):
    out_hbm, state_hbm, out_ref, sems = refs
    chunks = sems.shape[0] - 1
    store = pltpu.make_async_copy(state_ref, state_hbm, sems.at[chunks])
    store.start()
    square = mine_ref[...] + other_ref[...]
    scale = 1.0 / jnp.sqrt(square / total_width + 1e-05)
    width = out_ref.shape[1] // chunks
    stores = [store]
    for chunk in range(chunks):
        for start in range(chunk * width, (chunk + 1) * width, LANES):
            lanes = slice(start, start + LANES)
            out_ref[:, lanes] = (mixed_ref[:, lanes] * scale * gain_ref[:, lanes]).astype(BF16)
        view = pl.ds(chunk * width, width)
        stores.append(
            pltpu.make_async_copy(out_ref.at[:, view], out_hbm.at[:, view], sems.at[chunk])
        )
        stores[-1].start()
    for store in stores:
        store.wait()


SPACES = {"h": pltpu.HBM, "v": pltpu.VMEM, "s": pltpu.SMEM}


def call(body, ins, outs, scratch=(), mebibytes=8):
    def run(*operands):
        placed = [
            operand if space == "s" else pltpu.with_memory_space_constraint(operand, SPACES[space])
            for space, operand in zip(ins, operands, strict=True)
        ]
        return pl.pallas_call(
            body,
            out_shape=tuple(SPACES[space](dims, kind) for space, dims, kind in outs),
            in_specs=[pl.BlockSpec(memory_space=SPACES[space]) for space in ins],
            out_specs=tuple(pl.BlockSpec(memory_space=SPACES[out[0]]) for out in outs),
            scratch_shapes=scratch,
            compiler_params=pltpu.CompilerParams(vmem_limit_bytes=mebibytes * 1024 * 1024),
        )(*placed)

    return run


def local(
    draft_input,
    draft_proj,
    draft_step,
    draft_query,
    draft_keyval,
    row_target,
    tree_mask,
    accepted,
    cache_length,
    scan_state,
    cache_keyval,
    decay_rate,
    step_bias,
    skip_gain,
    norm_gain,
):
    row_count, scan_width = draft_input.shape
    peers = lax.axis_size("req")
    head_shards = lax.axis_size("head")
    cap_rows = max(2, row_count // peers)
    slot_total = peers * cap_rows
    direct = peers == len(EARLY_FROM)
    assert row_count & (row_count - 1) == 0 and scan_width * 2 == LANES * HEAD_DIM
    head_local = scan_width // HEAD_DIM
    query_width = draft_query.shape[1]
    keyval_width = draft_keyval.shape[1]
    proj_width = draft_proj.shape[1]
    groups = proj_width // (2 * STATE)
    all_width = scan_width + query_width + keyval_width + proj_width + LANES
    late = 0
    if direct:
        odd = range(1, peers, 2)
        even = range(2, peers, 2)
        unit = scan_width // 8
        early_from = [EARLY_FROM[block] * unit for block in range(peers)]
        layout = [((0, 1, 0, all_width, 0),)]
        layout += [((block, 1, early_from[block], all_width, 0),) for block in range(2, peers)]
        layout += [((block, 1, 0, early_from[block], 0),) for block in even]
        side, side_width = [(1, 1, 0, all_width, 0)], all_width
        for block in odd[1:]:
            side.append((block, 1, 0, early_from[block], side_width))
            side_width += early_from[block]
        layout += [tuple(side)]
        widths = [all_width] + [all_width - early_from[block] for block in range(2, peers)]
        widths += [max(early_from[block], LANES) for block in even] + [side_width]
        rows_of = cap_rows
    else:
        layout, widths = [((0, peers, 0, all_width, 0),)], [all_width]
        rows_of = slot_total
    sources = (draft_input, draft_query, draft_keyval, draft_proj, draft_step)
    packed = call(
        functools.partial(pack, (row_count, cap_rows, peers), direct, layout),
        "h" * 6,
        tuple(("v", (rows_of, width), BF16) for width in widths),
        scratch=[pltpu.VMEM((1, row_count), jnp.int32)]
        + [pltpu.VMEM(source.shape, BF16) for source in sources]
        + [pltpu.SemaphoreType.DMA((6,))],
    )(row_target.reshape(1, row_count), *sources)

    def moved(block, step):
        pairs = [(index, index ^ step) for index in range(peers)]
        return lax.ppermute(block, "req", pairs)

    if direct:
        own, rest, inputs = packed[0], packed[1 : peers - 1], packed[peers - 1 :]
        arrived = moved(inputs[-1], 1)
        rest = [moved(block, step) for step, block in enumerate(rest, start=2)]
        later = [block for block in even if early_from[block] + early_from[block + 1]]
        inputs = {block: part for block, part in zip(even, inputs)}
        count = len(later)

        def forward_all(accepted_ref, length_ref, *refs):
            widths = [(early_from[block], early_from[block + 1]) for block in later]
            skips = [sum(early_from[3:block:2]) for block in later]
            forward(widths, refs[count], [all_width + skip for skip in skips], refs[:count], refs[count + 1 : -1])
            lane = lax.broadcasted_iota(jnp.int32, refs[-1].shape, 1)
            refs[-1][...] = jnp.where(lane == 0, accepted_ref[0], length_ref[0])

        *pairs, scalars = call(
            forward_all,
            "ss" + "v" * (count + 1),
            tuple(
                ("v", (cap_rows, early_from[block] + early_from[block + 1]), BF16)
                for block in later
            )
            + (("v", (8, LANES), jnp.int32),),
        )(accepted, cache_length, *[inputs[block] for block in later], arrived)
        pairs = {block: moved(part, block) for block, part in zip(later, pairs)}
        first_blocks, first_offsets = [own, arrived] + rest, [0, 0] + early_from[2:]
        second_blocks, second_offsets = [own, arrived], [0, 0]
        for step in even:
            block = pairs.get(step, own)
            second_blocks += [block, block]
            second_offsets += [0, -early_from[step]]
        late = early_from
    else:
        split = packed[0].reshape(peers, cap_rows, all_width)
        arrived = lax.all_to_all(split, "req", split_axis=0, concat_axis=0, tiled=True)
        first_blocks, first_offsets = [arrived.reshape(slot_total, all_width)], [0]
        scalars = lax.pad(accepted, 0, [(0, LANES - 1, 0)])
        scalars = scalars + lax.pad(cache_length, 0, [(1, LANES - 2, 0)])
        scalars = jnp.broadcast_to(scalars, (8, LANES))
        second_blocks, second_offsets = [], []

    pair_heads = keyval_width // (2 * QDIM)
    score_rows = NODES * (query_width // QDIM // pair_heads)
    key_rows = cache_keyval.shape[1] + LANES
    attended, weight, base, columns, keep, write, order, skip_wide, gain, state = call(
        functools.partial(
            middle,
            first_offsets,
            (query_width, keyval_width, proj_width, head_local, scan_width),
        ),
        "v" * (len(first_blocks) + 1) + "h" * 7,
        (
            ("v", (row_count, query_width), BF16),
            ("v", (NODES, head_local * NODES), BF16),
            ("v", (NODES, scan_width), F32),
            ("v", (NODES, LANES), F32),
            ("v", (head_local, LANES), F32),
            ("v", (NODES, groups * STATE), BF16),
            ("v", (NODES, slot_total), BF16),
            ("v", (1, scan_width), F32),
            ("v", (1, scan_width), F32),
            ("v", scan_state.shape, BF16),
        ),
        scratch=[
            pltpu.VMEM(tree_mask.shape, jnp.int32),
            pltpu.VMEM((1, head_local), F32),
            pltpu.VMEM((1, head_local), F32),
            pltpu.VMEM((1, head_local), F32),
            pltpu.VMEM((pair_heads, key_rows, QDIM), BF16),
            pltpu.VMEM((pair_heads, key_rows, QDIM), BF16),
            pltpu.VMEM((pair_heads, score_rows, QDIM), BF16),
            pltpu.VMEM((pair_heads, score_rows, key_rows), F32),
            pltpu.VMEM((pair_heads, score_rows, key_rows), BF16),
            pltpu.VMEM((pair_heads, score_rows, QDIM), F32),
            pltpu.VMEM((2, head_local, LANES), F32),
            pltpu.SemaphoreType.DMA((6 + 2 * pair_heads,)),
        ],
        mebibytes=28,
    )(
        *first_blocks,
        scalars,
        tree_mask,
        decay_rate.reshape(1, head_local),
        step_bias.reshape(1, head_local),
        skip_gain.reshape(1, head_local),
        scan_state,
        cache_keyval,
        norm_gain.reshape(1, scan_width),
    )

    mixed, square, inputs, attend_out = call(
        functools.partial(mix, first_offsets, second_offsets, late),
        "v" * (len(first_blocks) + len(second_blocks) + 5),
        (
            ("v", (NODES, scan_width), F32),
            ("v", (NODES, LANES), F32),
            ("v", (NODES, scan_width), BF16),
            ("h", (row_count, query_width), BF16),
        ),
        scratch=[pltpu.SemaphoreType.DMA(())],
    )(*first_blocks, *second_blocks, order, weight, base, skip_wide, attended)
    swap = [(index, (index + 1) % head_shards) for index in range(head_shards)]
    other = lax.ppermute(square, "head", swap)
    new_state = call(advance, "v" * 5, (("v", scan_state.shape, BF16),))(
        inputs, columns, write, keep, state
    )[0]
    mixer_out, new_state = call(
        functools.partial(finish, head_shards * scan_width),
        "v" * 5,
        (("h", (row_count, scan_width), BF16), ("h", scan_state.shape, BF16)),
        scratch=[pltpu.VMEM((row_count, scan_width), BF16), pltpu.SemaphoreType.DMA((5,))],
    )(mixed, square, other, gain, new_state)
    return (mixer_out, attend_out, new_state)


def solution(mesh):
    assert mesh.shape["head"] == 2
    rows = P(("grp", "req"), "head")

    return jax.shard_map(
        local,
        mesh=mesh,
        in_specs=(
            rows,
            rows,
            rows,
            rows,
            rows,
            P(("grp", "req")),
            P(("grp", "req"), None, None),
            P(("grp", "req")),
            P(("grp", "req")),
            P(("grp", "req"), "head", None, None),
            P(("grp", "req"), None, "head"),
            P("head"),
            P("head"),
            P("head"),
            P("head"),
        ),
        out_specs=(rows, rows, P(("grp", "req"), "head", None, None)),
        check_vma=False,
    )
```
